32 devices in a mesh: region: 4 (over z), tile: 8 (over y, x, core).
Axes of the slice: x: 2, y: 2, z: 4, core: 2. Of those that a mesh axis runs over, the one named last changes fastest.
Arguments:
- movie: bfloat16 [131072, 256], P(('region', 'tile'))
- footprint: float32 [8192, 128], P(('region', 'tile')), may hold values from 0.05 to 1
- support_idx: int32 [8192, 128], P(('region', 'tile')), may hold values from 0 to 4095
- trace_old: float32 [8192, 256], P(('region', 'tile')), may hold values from 0 to 7.5
- ar_coef: float32 [2], replicated, as said below
- border_fp: float32 [1536, 128], P(('region', 'tile')), may hold values from 0.05 to 1
- border_idx: int32 [1536, 128], P(('region', 'tile')), may hold values from 0 to 4095
- border_owner: int32 [1536], P(('region', 'tile')), may hold values from 0 to 255
- border_offset: int32 [1536, 1], P(('region', 'tile')), may hold values from 0 to 6; in each aligned block of 48 rows (0 to 47, 48 to 95, ...) at most 8 rows name the same one
- back_spatial: float32 [131072], P(('region', 'tile')), may hold values from 0.1 to 1
- back_trace: float32 [256], replicated, may hold values from 0.5 to 1.5
Outputs:
- trace_new: float32 [8192, 256], P(('region', 'tile'))
- footprint_new: float32 [8192, 128], P(('region', 'tile'))
- border_new: float32 [1536, 128], P(('region', 'tile'))
- back_new: float32 [256], replicated
The draws below stay inside these ranges and needn't reach their ends.
Inputs may be any that keep to these rules, and one draw needn't show every extreme that they name: `border_offset`: in the rows of one tile at most 8 border rows name the same offset, a bound that some block reaches. ar_coef = (p + r, -p r) with slow root p and fast root r.
All inputs are finite; a program needn't handle non-finite values.
Results may differ from the reference program's by a relative error of at most 0.0081.
The reference program's roundings to bfloat16 on the way (of `dense_own`, `resid` and `resid2`) count: a program that leaves them out, or rounds other values in their place, can miss the bound.
Values sent between devices are 32-bit elements; how exact they have to be, the bound alone decides.
No kernel may reach another device: no remote copies, remote signals or barrier semaphores. Data moves between devices by JAX's collectives and lax.ppermute only.
A program may use at most 64 MiB of HBM per device.

```python
import math
import jax
import jax.numpy as jnp
import numpy as np
from jax import lax

RECORDING_STEPS = 256
VOX_DEV = 4096
K_DEV = 256
SUP = 128
BORDER = 48
BSUP = 128
CAP = 8
VOXELS = 131072
CELL_COUNT = 8192
BORDERS = 1536
N_REGION = 4
N_TILE = 8


def decay_roots(key):
    key_slow, key_fast = jax.random.split(jax.random.fold_in(key, 11))
    slow_root = jax.random.uniform(key_slow, (), jnp.float32, 0.7, 0.9)
    fast_root = jax.random.uniform(key_fast, (), jnp.float32, 0.05, 0.4)
    return (slow_root + fast_root, -slow_root * fast_root)


def draw_ar_coef(key, part):
    prior_step_weight, earlier_step_weight = decay_roots(key)
    return jnp.stack([prior_step_weight, earlier_step_weight]).astype(jnp.float32)


def footprint_values(key):
    return jax.random.uniform(jax.random.fold_in(key, 21), (CELL_COUNT, SUP), jnp.float32, 0.05, 1.0)


def draw_footprint(key, part):
    return footprint_values(key)


def support_voxels(key):
    return jax.random.randint(jax.random.fold_in(key, 22), (CELL_COUNT, SUP), 0, VOX_DEV, dtype=jnp.int32)


def draw_support_idx(key, part):
    return support_voxels(key)


def spatial_profile(key):
    exponent = jax.random.uniform(jax.random.fold_in(key, 24), (VOXELS,), jnp.float32, math.log(0.1), math.log(1.0))
    return jnp.clip(jnp.exp(exponent), 0.1, 1.0).astype(jnp.float32)


def draw_back_spatial(key, part):
    return spatial_profile(key)


def temporal_profile(key):
    return jax.random.uniform(jax.random.fold_in(key, 25), (RECORDING_STEPS,), jnp.float32, 0.5, 1.5)


def draw_back_trace(key, part):
    return temporal_profile(key)


def calcium_traces(key):
    prior_step_weight, earlier_step_weight = decay_roots(key)
    discharge_intensity = (jax.random.randint(jax.random.fold_in(key, 23), (RECORDING_STEPS, CELL_COUNT), 0, 5, dtype=jnp.int32) == 0).astype(jnp.float32)
    pulse_amplitude = jax.random.uniform(jax.random.fold_in(key, 27), (RECORDING_STEPS, CELL_COUNT), jnp.float32, 0.5, 1.5)
    action_potentials = discharge_intensity * pulse_amplitude * (5.0 * (1.0 - prior_step_weight - earlier_step_weight))

    def advance(carry, event):
        prev_one, prev_two = carry
        current = event + prior_step_weight * prev_one + earlier_step_weight * prev_two
        return ((current, prev_one), current)
    initial = jnp.zeros((CELL_COUNT,), jnp.float32)
    unused, levels = lax.scan(advance, (initial, initial), action_potentials)
    return levels.T


def draw_trace_old(key, part):
    return calcium_traces(key)


def draw_movie(key, part):
    tile_count = CELL_COUNT // K_DEV
    values = footprint_values(key)
    voxels = support_voxels(key)
    traces = calcium_traces(key)
    spatial = spatial_profile(key)
    temporal = temporal_profile(key)
    prior_step_weight, earlier_step_weight = decay_roots(key)

    def tile_signal(items):
        tile_values, tile_voxels, tile_traces = items
        columns = jnp.broadcast_to(jnp.arange(K_DEV, dtype=jnp.int32)[:, None], tile_voxels.shape)
        dense_grid = jnp.zeros((VOX_DEV, K_DEV), jnp.float32)
        dense_grid = dense_grid.at[tile_voxels.reshape(-1), columns.reshape(-1)].add(tile_values.reshape(-1))
        return jnp.dot(dense_grid, tile_traces, precision=lax.Precision.HIGHEST)
    signal = lax.map(tile_signal, (values.reshape(tile_count, K_DEV, SUP), voxels.reshape(tile_count, K_DEV, SUP), traces.reshape(tile_count, K_DEV, RECORDING_STEPS)))
    signal = signal.reshape(VOXELS, RECORDING_STEPS)
    brightness = jax.random.uniform(jax.random.fold_in(key, 28), (tile_count,), jnp.float32, 0.7, 1.4)
    voxel_bright = jnp.repeat(brightness, VOX_DEV) * spatial
    mean_event = 1.0 - prior_step_weight - earlier_step_weight

    def advance_mean(carry, unused_step):
        prev_one, prev_two = carry
        current = mean_event + prior_step_weight * prev_one + earlier_step_weight * prev_two
        return ((current, prev_one), current)
    anchor = jnp.zeros((), jnp.float32)
    unused, mean_trace = lax.scan(advance_mean, (anchor, anchor), None, length=RECORDING_STEPS)
    border_level = BORDER * BSUP / VOX_DEV * 0.525 * mean_trace
    jitter = 0.2 * jax.random.truncated_normal(jax.random.fold_in(key, 26), -3.0, 3.0, (VOXELS, RECORDING_STEPS), jnp.float32)
    recorded = signal + voxel_bright[:, None] * temporal[None, :] + border_level[None, :] + jitter
    return recorded.astype(jnp.bfloat16)


def touch_ends(values, own_key, smallest, high):
    extent = values.shape
    index_at = [jax.random.randint(jax.random.fold_in(own_key, axis), (), 0, extent[axis]) for axis in range(len(extent))]
    values = values.at[tuple(index_at)].set(smallest)
    longest = extent.index(max(extent))
    index_at[longest] = (index_at[longest] + 1) % extent[longest]
    return values.at[tuple(index_at)].set(high)


def level_of(rng, shape, cuts, smallest, largest):
    def one(dim, shards_of):
        steps = jax.random.uniform(jax.random.fold_in(jax.random.fold_in(rng, 6), dim), (shards_of,), jnp.float32, smallest / len(cuts), largest / len(cuts))
        return jnp.repeat(jnp.exp(steps), shape[dim] // shards_of).reshape((-1,) + (1,) * (len(shape) - dim - 1))

    level = one(*cuts[0])
    for cut in cuts[1:]:
        level = level * one(*cut)
    return level


def shared_out(key, own, number, rows, count, top, limit, slope):
    order = jax.random.permutation(key, count)
    packed, usual = shares(count, rows * top, limit, slope, True), shares(count, rows * top, limit, slope, False)
    places = jnp.arange(count)

    def named(tallies, rotation):
        used = int((tallies > 0).sum())
        fixed = max(1, used // 4)
        moved = fixed + (places - fixed + rotation * (used - fixed)) % max(1, count - fixed)
        return jnp.zeros((count,), jnp.int32).at[order[jnp.where(places < fixed, places, moved)]].set(jnp.asarray(tallies, jnp.int32))

    tallies = jnp.where(number % 4 == 0, named(packed, number // 4), named(usual, number - number // 4 - 1))
    mixed = jax.random.permutation(jax.random.fold_in(own, 3), count)
    source_of, taker = mixed[0:count // 2 * 2:2], mixed[1:count // 2 * 2:2]
    slack = jnp.minimum(tallies[source_of] - 1, limit - tallies[taker]) // 2
    slack = jnp.where((source_of == order[0]) | (taker == order[0]) | (tallies[taker] == 0), 0, jnp.maximum(slack, 0))
    moved = jax.random.randint(jax.random.fold_in(own, 4), (count // 2,), 0, 1 << 20) % (slack + 1)
    tallies = tallies.at[source_of].add(-moved).at[taker].add(moved)
    members = jnp.searchsorted(jnp.cumsum(tallies), jnp.arange(rows * top), side="right").astype(jnp.int32)
    table = members.reshape(top, rows).T
    table = table[jax.random.permutation(jax.random.fold_in(own, 1), rows)]
    rotation = jax.random.randint(jax.random.fold_in(own, 2), (rows, 1), 0, top)
    return jnp.take_along_axis(table, (jnp.arange(top)[None, :] + rotation) % top, axis=1)


def shares(number_of, total, reach, skew, full):
    portions = [(1 << 20) // math.isqrt(standing ** skew) + 1 for standing in range(1, number_of + 1)]
    largest = reach if full else min(reach, max(-(-total // number_of), total * portions[0] // sum(portions)))
    least = 1 if total - largest >= number_of - 1 else 0
    counts, surplus = [largest] + [least] * (number_of - 1), total - largest - least * (number_of - 1)
    while surplus > 0:
        movable = [i for i in range(1, number_of) if counts[i] < largest] or [i for i in range(1, number_of) if counts[i] < reach]
        pool, remaining = sum([portions[i] for i in movable]), surplus
        for i in movable:
            addition = min(reach - counts[i], max(1, remaining * portions[i] // pool), surplus)
            counts[i] = counts[i] + addition
            surplus = surplus - addition
    return np.array(counts)


def setup_inputs(seed: int = 0) -> dict:
    keys = jax.random.split(jax.random.key(seed), 12)
    movie = draw_movie(jax.random.fold_in(keys[11], 71), 0)
    footprint = draw_footprint(jax.random.fold_in(keys[11], 71), 0)
    support_idx = draw_support_idx(jax.random.fold_in(keys[11], 71), 0)
    trace_old = draw_trace_old(jax.random.fold_in(keys[11], 71), 0)
    ar_coef = draw_ar_coef(jax.random.fold_in(keys[11], 71), 0)
    border_fp = jnp.clip(0.05 + 0.95 * jax.random.uniform(keys[5], (BORDERS, BSUP), jnp.float32) ** level_of(keys[5], (BORDERS, BSUP), ((0, 32),), -0.2, 0.2), 0.05, 1.0)
    border_idx = touch_ends(jax.random.randint(keys[6], (BORDERS, BSUP), 0, VOX_DEV), jax.random.fold_in(keys[6], 1), 0, VOX_DEV - 1).astype(jnp.int32)
    border_owner = touch_ends(jax.random.randint(keys[7], (BORDERS,), 0, K_DEV), jax.random.fold_in(keys[7], 1), 0, K_DEV - 1).astype(jnp.int32)
    border_offset_keys = jax.random.split(jax.random.fold_in(keys[8], 1), BORDERS // BORDER)
    border_offset_turns = jax.random.permutation(jax.random.fold_in(keys[8], 3), BORDERS // BORDER)
    border_offset = jax.vmap(lambda own, number: shared_out(jax.random.fold_in(keys[8], 2), own, number, BORDER, N_TILE - 1, 1, CAP, 2))(border_offset_keys, border_offset_turns).reshape((BORDERS, 1))
    back_spatial = draw_back_spatial(jax.random.fold_in(keys[11], 71), 0)
    back_trace = draw_back_trace(jax.random.fold_in(keys[11], 71), 0)
    return {"movie": movie, "footprint": footprint, "support_idx": support_idx, "trace_old": trace_old, "ar_coef": ar_coef, "border_fp": border_fp, "border_idx": border_idx, "border_owner": border_owner, "border_offset": border_offset, "back_spatial": back_spatial, "back_trace": back_trace}


RIDGE = 1.0
EXACT = lax.Precision.HIGHEST


def slot_table(own_tile, offsets, tile_count, capacity):
    target = (own_tile + 1 + offsets) % tile_count
    target_hits = (target[:, None] == jnp.arange(tile_count, dtype=jnp.int32)[None, :]).astype(jnp.int32)
    bucket_rank = jnp.sum((jnp.cumsum(target_hits, axis=0) - target_hits) * target_hits, axis=1)
    slot_index = (target * capacity + bucket_rank).astype(jnp.int32)
    slot_range = jnp.arange(tile_count * capacity, dtype=jnp.int32)
    return (slot_index[:, None] == slot_range[None, :]).astype(jnp.float32)


def dense_map(values, places, voxel_count):
    row_count = values.shape[0]
    columns = jnp.broadcast_to(jnp.arange(row_count, dtype=jnp.int32)[:, None], places.shape)
    dense_grid = jnp.zeros((voxel_count, row_count), jnp.float32)
    dense_grid = dense_grid.at[places.reshape(-1), columns.reshape(-1)].add(values.reshape(-1))
    return dense_grid.astype(jnp.bfloat16)


def impulse_matrix(ar_coef, frame_count):
    prior_step_weight = ar_coef[0]
    earlier_step_weight = ar_coef[1]
    response = [jnp.ones((), jnp.float32), prior_step_weight]
    for position in range(2, frame_count):
        response.append(prior_step_weight * response[-1] + earlier_step_weight * response[-2])
    impulse = jnp.stack(response[:frame_count])
    later = jnp.arange(frame_count, dtype=jnp.int32)[:, None]
    earlier = jnp.arange(frame_count, dtype=jnp.int32)[None, :]
    offset = jnp.clip(later - earlier, 0, frame_count - 1)
    return jnp.where(later >= earlier, impulse[offset], jnp.zeros((), jnp.float32))


def whiten(trace_in, ar_coef):
    prev_one = jnp.pad(trace_in, ((0, 0), (1, 0)))[:, :-1]
    prev_two = jnp.pad(trace_in, ((0, 0), (2, 0)))[:, :-2]
    return trace_in - ar_coef[0] * prev_one - ar_coef[1] * prev_two


def swap_tiles(array):
    slots = N_TILE * CAP
    shaped = array.reshape((N_REGION, N_TILE, N_TILE, CAP) + array.shape[2:])
    shaped = jnp.swapaxes(shaped, 1, 2)
    return shaped.reshape((N_REGION * N_TILE, slots) + array.shape[2:])


def reconstruct(dense_own, dense_in, trace_own, trace_in):
    first = jnp.dot(dense_own, trace_own.astype(jnp.bfloat16), preferred_element_type=jnp.float32)
    return first + jnp.dot(dense_in.astype(jnp.float32), trace_in, precision=EXACT)


def reference(movie, footprint, support_idx, trace_old, ar_coef, border_fp, border_idx, border_owner, border_offset, back_spatial, back_trace):
    devs = N_REGION * N_TILE
    movie_d = movie.reshape(devs, VOX_DEV, RECORDING_STEPS)
    fp_d = footprint.reshape(devs, K_DEV, SUP)
    idx_d = support_idx.reshape(devs, K_DEV, SUP)
    old_d = trace_old.reshape(devs, K_DEV, RECORDING_STEPS)
    bfp_d = border_fp.reshape(devs, BORDER, BSUP)
    bidx_d = border_idx.reshape(devs, BORDER, BSUP)
    bown_d = border_owner.reshape(devs, BORDER)
    boff_d = border_offset.reshape(devs, BORDER)
    spatial_d = back_spatial.reshape(devs, VOX_DEV)
    tile_of = (jnp.arange(devs, dtype=jnp.int32) % N_TILE).astype(jnp.int32)

    def make_table(items):
        return slot_table(items[0], items[1], N_TILE, CAP)

    place = lax.map(make_table, (tile_of, boff_d))
    send_fp = jnp.einsum("dbs,dbj->dsj", place, bfp_d, precision=EXACT)
    send_idx = jnp.einsum("dbs,dbj->dsj", place, bidx_d.astype(jnp.float32), precision=EXACT)
    send_old = jnp.einsum("dbs,dbf->dsf", place, jnp.take_along_axis(old_d, bown_d[:, :, None], axis=1), precision=EXACT)
    send_owner = jnp.einsum("dbs,db->ds", place, bown_d.astype(jnp.float32), precision=EXACT)
    in_fp = swap_tiles(send_fp)
    in_idx = swap_tiles(send_idx).astype(jnp.int32)
    in_old = swap_tiles(send_old)
    in_owner = swap_tiles(send_owner).astype(jnp.int32)

    def section_project(items):
        movie_tile, fp_tile, idx_tile, old_tile, infp, inidx, inold, spatial = items
        dense_own = dense_map(fp_tile, idx_tile, VOX_DEV)
        dense_in = dense_map(infp, inidx, VOX_DEV)
        recon = reconstruct(dense_own, dense_in, old_tile, inold) + spatial[:, None] * back_trace[None, :]
        resid = (movie_tile.astype(jnp.float32) - recon).astype(jnp.bfloat16)
        dims = (((0,), (0,)), ((), ()))
        proj_own = lax.dot_general(dense_own, resid, dims, preferred_element_type=jnp.float32)
        proj_in = lax.dot_general(dense_in, resid, dims, preferred_element_type=jnp.float32)
        return proj_own, proj_in

    proj_own, proj_in = lax.map(section_project, (movie_d, fp_d, idx_d, old_d, in_fp, in_idx, in_old, spatial_d))
    returned = swap_tiles(proj_in)
    mine = jnp.einsum("dbs,dsf->dbf", place, returned, precision=EXACT)
    owner_hot = (bown_d[:, :, None] == jnp.arange(K_DEV, dtype=jnp.int32)[None, None, :]).astype(jnp.float32)
    gain = proj_own + jnp.einsum("dbk,dbf->dkf", owner_hot, mine, precision=EXACT)
    energy = jnp.sum(fp_d * fp_d, axis=2) + jnp.einsum("dbk,db->dk", owner_hot, jnp.sum(bfp_d * bfp_d, axis=2), precision=EXACT)
    raw = old_d + gain / energy[:, :, None]
    spikes = jnp.maximum(whiten(raw.reshape(devs * K_DEV, RECORDING_STEPS), ar_coef), 0.0)
    inverse = impulse_matrix(ar_coef, RECORDING_STEPS)
    trace_flat = jnp.dot(spikes, inverse.T, precision=EXACT)
    trace_d = trace_flat.reshape(devs, K_DEV, RECORDING_STEPS)

    region_of = jnp.arange(devs, dtype=jnp.int32) // N_TILE
    source = jnp.arange(N_TILE * CAP, dtype=jnp.int32) // CAP
    rows = ((region_of[:, None] * N_TILE + source[None, :]) * K_DEV + in_owner).astype(jnp.int32)
    in_new = jnp.take(trace_flat, rows.reshape(-1), axis=0).reshape(devs, N_TILE * CAP, RECORDING_STEPS)

    def section_rest(items):
        movie_tile, fp_tile, idx_tile, new_tile, infp, inidx, innew, spatial = items
        dense_own = dense_map(fp_tile, idx_tile, VOX_DEV)
        dense_in = dense_map(infp, inidx, VOX_DEV)
        rest = movie_tile.astype(jnp.float32) - reconstruct(dense_own, dense_in, new_tile, innew)
        return jnp.dot(spatial, rest, precision=EXACT)

    section_items = (movie_d, fp_d, idx_d, trace_d, in_fp, in_idx, in_new, spatial_d)
    partial_sums = lax.map(section_rest, section_items)
    back_new = jnp.sum(partial_sums, axis=0) / jnp.sum(back_spatial * back_spatial)

    def section_update(items):
        movie_tile, fp_tile, idx_tile, new_tile, infp, inidx, innew, spatial = items
        dense_own = dense_map(fp_tile, idx_tile, VOX_DEV)
        dense_in = dense_map(infp, inidx, VOX_DEV)
        rest = movie_tile.astype(jnp.float32) - reconstruct(dense_own, dense_in, new_tile, innew)
        resid2 = (rest - spatial[:, None] * back_new[None, :]).astype(jnp.bfloat16)
        dims = (((1,), (1,)), ((), ()))
        grad_own = lax.dot_general(new_tile.astype(jnp.bfloat16), resid2, dims, preferred_element_type=jnp.float32)
        grad_in = lax.dot_general(innew.astype(jnp.bfloat16), resid2, dims, preferred_element_type=jnp.float32)
        denom_own = jnp.sum(new_tile * new_tile, axis=1) + RIDGE
        denom_in = jnp.sum(innew * innew, axis=1) + RIDGE
        fp_next = jnp.maximum(fp_tile + jnp.take_along_axis(grad_own, idx_tile, axis=1) / denom_own[:, None], 0.0)
        in_next = jnp.maximum(infp + jnp.take_along_axis(grad_in, inidx, axis=1) / denom_in[:, None], 0.0)
        return fp_next, in_next

    fp_next, in_next = lax.map(section_update, section_items)
    back_rows = swap_tiles(in_next)
    border_next = jnp.einsum("dbs,dsj->dbj", place, back_rows, precision=EXACT)
    return (trace_flat, fp_next.reshape(devs * K_DEV, SUP), border_next.reshape(devs * BORDER, BSUP), back_new)
```

```python
import jax
import jax.numpy as jnp
from jax import lax
from jax.experimental import pallas as pl
from jax.experimental.pallas import tpu as pltpu
from jax.sharding import PartitionSpec as P

CAP = 8
RIDGE = 1.0
LANES = 128
F32 = jnp.float32
BF16 = jnp.bfloat16
VMEM_BYTES = 28 << 20
CHUNK = 512


def nn(a, b):
    return lax.dot_general(a, b, (((1,), (0,)), ((), ())), preferred_element_type=F32)


def nt(a, b):
    return lax.dot_general(a, b, (((1,), (1,)), ((), ())), preferred_element_type=F32)


def split(x, terms):
    parts = []
    for _ in range(terms):
        part = x.astype(BF16)
        parts.append(part)
        x = x - part.astype(F32)
    return parts


def select_rows(table, x, terms=3):
    total = None
    for part in reversed(split(x, terms)):
        term = nn(table, part)
        total = term if total is None else total + term
    return total


def iota(shape, dim):
    return lax.broadcasted_iota(jnp.int32, shape, dim)


def to_column(row):
    n = row.shape[1]
    return jnp.sum(jnp.where(iota((n, n), 0) == iota((n, n), 1), row, jnp.zeros_like(row)), axis=1, keepdims=True)


def shift_lanes(x, count):
    return jnp.where(iota(x.shape, len(x.shape) - 1) >= count, pltpu.roll(x, count, len(x.shape) - 1), 0.0)


def pack_kernel(tile_ref, bfp_ref, bidx_ref, bown_ref, boff_ref, old_ref, send_ref, pick_ref, pick_t_ref, place_ref):
    tiles = send_ref.shape[0] // CAP
    slots = send_ref.shape[0]
    border = bfp_ref.shape[0]
    owned = old_ref.shape[0]
    support = bfp_ref.shape[1]
    target = boff_ref[...] + (tile_ref[0] + 1)
    target = jnp.where(target >= tiles, target - tiles, target)
    target_col = to_column(target)
    same = target_col == target
    before = iota((border, border), 0) < iota((border, border), 1)
    rank = jnp.sum(jnp.where(jnp.logical_and(same, before), 1, 0), axis=0, keepdims=True)
    slot = target * CAP + rank
    owner = bown_ref[...]
    place_t = iota((slots, border), 0) == slot
    place = iota((border, slots), 1) == to_column(slot)
    owner_col = jnp.sum(jnp.where(place_t, owner + 1, 0), axis=1, keepdims=True) - 1
    owner_row = jnp.sum(jnp.where(place, to_column(owner) + 1, 0), axis=0, keepdims=True) - 1
    pick = jnp.where(iota((slots, owned), 1) == owner_col, 1.0, 0.0).astype(BF16)
    pick_ref[...] = pick
    pick_t_ref[...] = jnp.where(iota((owned, slots), 0) == owner_row, 1.0, 0.0).astype(BF16)
    place_ref[...] = jnp.where(place, 1.0, 0.0).astype(BF16)
    place_t = jnp.where(place_t, 1.0, 0.0).astype(BF16)
    send_ref[:, :support] = select_rows(place_t, bfp_ref[...])
    send_ref[:, support:2 * support] = select_rows(place_t, bidx_ref[...].astype(F32), 2)
    send_ref[:, 2 * support:] = select_rows(pick, old_ref[...])


def scatter_rows(values_ref, index_ref, grid_ref, rows):
    cells = grid_ref.shape[0] // rows
    support = values_ref.shape[1]
    hi_range = iota((cells, support), 0).astype(BF16)
    lo_range = iota((LANES, support), 0).astype(BF16)
    zero_lo = jnp.zeros((LANES, support), BF16)

    def one(row):
        index = index_ref[pl.ds(row, 1), :]
        value = values_ref[pl.ds(row, 1), :]
        high = jnp.broadcast_to((index >> 7).astype(F32), (cells, support)).astype(BF16)
        low = jnp.broadcast_to((index & 127).astype(F32), (LANES, support)).astype(BF16)
        coarse = value.astype(BF16).astype(F32)
        fine = value - coarse
        top = jnp.broadcast_to(coarse, (LANES, support)).astype(BF16)
        rest = jnp.broadcast_to(fine, (LANES, support)).astype(BF16)
        hit = low == lo_range
        left = jnp.where(high == hi_range, jnp.ones((cells, support), BF16), jnp.zeros((cells, support), BF16))
        left = jnp.concatenate([left, left], axis=1)
        right = jnp.concatenate([jnp.where(hit, top, zero_lo), jnp.where(hit, rest, zero_lo)], axis=1)
        grid_ref[pl.ds(row, cells, stride=rows), :] = nt(left, right)

    @pl.loop(0, rows // 8)
    def _(group):
        for k in range(8):
            one(group * 8 + k)


def prepare_kernel(movie_ref, fp_ref, idx_ref, dense_ref, movie_t_ref, grid_ref):
    rows = fp_ref.shape[0]
    voxels, frames = movie_ref.shape
    scatter_rows(fp_ref, idx_ref, grid_ref, rows)

    @pl.loop(0, voxels // LANES)
    def _(cell):
        at = pl.multiple_of(cell * LANES, LANES)
        start = pl.multiple_of(cell * rows, rows)
        dense_ref[:, pl.ds(at, LANES)] = grid_ref[pl.ds(start, rows), :].astype(BF16)

    eye = jnp.where(iota((frames, frames), 0) == iota((frames, frames), 1), 1.0, 0.0).astype(BF16)

    @pl.loop(0, voxels // CHUNK)
    def _(step):
        at = pl.multiple_of(step * CHUNK, CHUNK)
        movie_t_ref[:, pl.ds(at, CHUNK)] = nt(eye, movie_ref[pl.ds(at, CHUNK), :]).astype(BF16)


def project_kernel(recv_ref, movie_t_ref, dense_ref, old_ref, spatial_ref, trace_ref, resid_ref, dense_in_ref, proj_ref, idx_ref, values_ref, grid_ref):
    slots = recv_ref.shape[0]
    frames, voxels = movie_t_ref.shape
    support = values_ref.shape[1]
    values_ref[...] = recv_ref[:, :support]
    idx_ref[...] = recv_ref[:, support:2 * support].astype(jnp.int32)
    scatter_rows(values_ref, idx_ref, grid_ref, slots)

    @pl.loop(0, voxels // LANES)
    def _(cell):
        at = pl.multiple_of(cell * LANES, LANES)
        start = pl.multiple_of(cell * slots, slots)
        part = grid_ref[pl.ds(start, slots), :].astype(BF16)
        for copy in range(3):
            dense_in_ref[copy * slots:(copy + 1) * slots, pl.ds(at, LANES)] = part

    old_t = jnp.transpose(old_ref[...]).astype(BF16)
    in_t = jnp.concatenate([jnp.transpose(part.astype(F32)).astype(BF16) for part in split(recv_ref[:, 2 * support:], 3)], axis=1)
    back = to_column(trace_ref[...])

    @pl.loop(0, voxels // CHUNK)
    def _(step):
        at = pl.multiple_of(step * CHUNK, CHUNK)
        here = pl.ds(at, CHUNK)
        recon = nn(old_t, dense_ref[:, here]) + nn(in_t, dense_in_ref[:, here]) + back * spatial_ref[:, here]
        resid_ref[:, here] = (movie_t_ref[:, here].astype(F32) - recon).astype(BF16)

    proj_ref[:, :frames] = nt(dense_in_ref[:slots, :], resid_ref[...])
    parts = jnp.concatenate(split(jnp.broadcast_to(spatial_ref[...], (8, voxels)), 3), axis=0)
    sums = nt(dense_in_ref[:slots, :], parts)
    proj_ref[:, frames:] = jnp.broadcast_to(sums[:, 0:1] + sums[:, 8:9] + sums[:, 16:17], (slots, LANES))


def own_kernel(ar_ref, dense_ref, resid_ref, movie_ref, spatial_ref, fp_ref, send_ref, pick_t_ref, proj_ref, energy_ref, weight_ref, base_ref, impulse_ref):
    frames, voxels = resid_ref.shape
    owned, support = fp_ref.shape
    proj_ref[...] = nt(dense_ref[...], resid_ref[...])
    spatial = spatial_ref[...]
    parts = jnp.concatenate(split(jnp.broadcast_to(spatial, (8, voxels)), 3), axis=0)
    sums = nt(dense_ref[...], parts)
    weight_ref[...] = jnp.broadcast_to(sums[:, 0:1] + sums[:, 8:9] + sums[:, 16:17], (owned, LANES))
    seen = nn(parts, movie_ref[...])
    seen = seen[0:8] + seen[8:16] + seen[16:24]
    norm = jnp.sum(spatial * spatial, axis=1, keepdims=True)
    row = iota((8, LANES), 0)
    base_ref[...] = jnp.where(row == 0, seen[:, :LANES], jnp.where(row == 1, seen[:, LANES:], jnp.where(row == 2, norm, 0.0)))
    border_fp = send_ref[:, :support]
    square = jnp.broadcast_to(jnp.sum(border_fp * border_fp, axis=1, keepdims=True), (send_ref.shape[0], LANES))
    fp = fp_ref[...]
    energy_ref[...] = jnp.sum(fp * fp, axis=1, keepdims=True) + select_rows(pick_t_ref[...], square)
    near, far = ar_ref[0], ar_ref[1]
    response = jnp.where(iota((8, frames), 1) == 0, 1.0, 0.0)
    step = 1
    while step < frames:
        change = near * shift_lanes(response, step)
        if 2 * step < frames:
            change = change - far * shift_lanes(response, 2 * step)
        response = response + change
        near, far = near * near + 2.0 * far, -far * far
        step *= 2
    wide = jnp.broadcast_to(response[0:1], (frames, frames))
    wide = pltpu.roll(wide, 0, 1, stride=1, stride_axis=0)
    impulse_ref[...] = jnp.where(iota((frames, frames), 1) >= iota((frames, frames), 0), wide, 0.0)


def trace_kernel(ar_ref, back_ref, proj_ref, energy_ref, weight_ref, base_ref, impulse_ref, old_ref, pick_ref, pick_t_ref, new_ref, send_ref):
    owned, frames = old_ref.shape
    returned = select_rows(pick_t_ref[...], back_ref[...])
    gain = proj_ref[...] + returned[:, :frames]
    raw = old_ref[...] + gain / energy_ref[:, 0:1]
    spikes = jnp.maximum(raw - ar_ref[0] * shift_lanes(raw, 1) - ar_ref[1] * shift_lanes(raw, 2), 0.0)
    new = jnp.dot(spikes, impulse_ref[...], precision=lax.Precision.HIGHEST, preferred_element_type=F32)
    new_ref[...] = new
    send_ref[:, :frames] = select_rows(pick_ref[...], new)
    used = weight_ref[:, 0:1] * new.astype(BF16).astype(F32) + returned[:, frames:frames + 1] * new
    used = jnp.sum(used, axis=0, keepdims=True)
    base = base_ref[...]
    row = iota((8, LANES), 0)
    base = base - jnp.where(row == 0, used[:, :LANES], jnp.where(row == 1, used[:, LANES:], 0.0))
    for tile in range(send_ref.shape[0] // CAP):
        send_ref[tile * CAP:(tile + 1) * CAP, frames:] = base


def rest_kernel(recv_ref, movie_t_ref, dense_ref, dense_in_ref, new_ref, rest_ref):
    frames, voxels = movie_t_ref.shape
    new_t = jnp.transpose(new_ref[...]).astype(BF16)
    in_t = jnp.concatenate([jnp.transpose(part.astype(F32)).astype(BF16) for part in split(recv_ref[:, :frames], 3)], axis=1)

    @pl.loop(0, voxels // CHUNK)
    def _(step):
        at = pl.multiple_of(step * CHUNK, CHUNK)
        here = pl.ds(at, CHUNK)
        recon = nn(new_t, dense_ref[:, here]) + nn(in_t, dense_in_ref[:, here])
        rest_ref[:, here] = movie_t_ref[:, here].astype(F32) - recon


def pick_support(grad_ref, idx_ref, out, rows):
    cells = grad_ref.shape[1] // LANES

    @pl.loop(0, rows // 8)
    def _(group):
        start = pl.multiple_of(group * 8, 8)
        here = pl.ds(start, 8)
        index = idx_ref[here, :]
        high = index >> 7
        low = index & 127
        picked = jnp.zeros(index.shape, F32)
        for cell in range(cells):
            found = jnp.take_along_axis(grad_ref[here, cell * LANES:(cell + 1) * LANES], low, axis=1, mode="promise_in_bounds")
            picked = jnp.where(high == cell, found, picked)
        out(here, picked)


def border_kernel(recv0_ref, recv_ref, *refs):
    *totals, spatial_ref, rest_ref, resid_ref, next_ref, back_ref, grad_ref, idx_ref, denom_ref = refs
    frames, voxels = rest_ref.shape
    slots, support = next_ref.shape
    total = totals[0][...]
    for other in totals[1:]:
        total = total + other[...]
    back = total[0:2] / total[2:3, 0:1]
    back_ref[...] = back
    back = to_column(jnp.concatenate([back[0:1], back[1:2]], axis=1))
    new = recv_ref[:, :frames]
    new_low = new.astype(BF16)

    @pl.loop(0, voxels // CHUNK)
    def _(step):
        at = pl.multiple_of(step * CHUNK, CHUNK)
        here = pl.ds(at, CHUNK)
        resid = (rest_ref[:, here] - back * spatial_ref[:, here]).astype(BF16)
        resid_ref[:, here] = resid
        grad_ref[:, here] = nn(new_low, resid)

    idx_ref[...] = recv0_ref[:, support:2 * support].astype(jnp.int32)
    denom_ref[...] = jnp.broadcast_to(jnp.sum(new * new, axis=1, keepdims=True) + RIDGE, (slots, support))

    def out(here, picked):
        next_ref[here, :] = jnp.maximum(recv0_ref[here, :support] + picked / denom_ref[here, :], 0.0)

    pick_support(grad_ref, idx_ref, out, slots)


def footprint_kernel(resid_ref, new_ref, fp_ref, idx_ref, out_ref, grad_ref, denom_ref):
    frames, voxels = resid_ref.shape
    owned, support = fp_ref.shape
    new = new_ref[...]
    new_low = new.astype(BF16)
    denom_ref[...] = jnp.broadcast_to(jnp.sum(new * new, axis=1, keepdims=True) + RIDGE, (owned, support))

    @pl.loop(0, voxels // CHUNK)
    def _(step):
        at = pl.multiple_of(step * CHUNK, CHUNK)
        here = pl.ds(at, CHUNK)
        grad_ref[:, here] = nn(new_low, resid_ref[:, here])

    def out(here, picked):
        out_ref[here, :] = jnp.maximum(fp_ref[here, :] + picked / denom_ref[here, :], 0.0)

    pick_support(grad_ref, idx_ref, out, owned)


def unpack_kernel(place_ref, rows_ref, out_ref):
    out_ref[...] = select_rows(place_ref[...], rows_ref[...])


def call(kernel, outs, scratch=(), name=None, smem=0, inputs=0, flops=0):
    specs = [pl.BlockSpec(memory_space=pltpu.SMEM)] * smem + [pl.BlockSpec(memory_space=pltpu.VMEM)] * (inputs - smem)
    many = len(outs) > 1
    shapes = [jax.ShapeDtypeStruct(s, d) for s, d in outs]
    return pl.pallas_call(
        kernel,
        out_shape=shapes if many else shapes[0],
        in_specs=specs,
        out_specs=[pl.BlockSpec(memory_space=pltpu.VMEM)] * len(outs) if many else pl.BlockSpec(memory_space=pltpu.VMEM),
        scratch_shapes=list(scratch),
        compiler_params=pltpu.CompilerParams(vmem_limit_bytes=VMEM_BYTES),
        name=name,
    )


def exchange(rows, tiles):
    width = rows.shape[1]
    moved = lax.all_to_all(rows.reshape(tiles, CAP, width), "tile", split_axis=0, concat_axis=0, tiled=True)
    return moved.reshape(tiles * CAP, width)


def body(movie, footprint, support_idx, trace_old, ar_coef, border_fp, border_idx, border_owner, border_offset, back_spatial, back_trace):
    tiles = lax.axis_size("tile")
    regions = lax.axis_size("region")
    tile = lax.axis_index("tile").astype(jnp.int32).reshape(1)
    voxels, frames = movie.shape
    owned, support = footprint.shape
    border = border_fp.shape[0]
    slots = tiles * CAP
    cells = voxels // LANES
    spatial = back_spatial.reshape(1, voxels)

    send, pick, pick_t, place = call(
        pack_kernel,
        [((slots, 2 * support + frames), F32), ((slots, owned), BF16), ((owned, slots), BF16), ((border, slots), BF16)],
        name="pack", smem=1, inputs=6,
    )(tile, border_fp, border_idx, border_owner.reshape(1, border), border_offset.reshape(1, border), trace_old)
    recv = exchange(send, tiles)
    dense, movie_t = call(
        prepare_kernel,
        [((owned, voxels), BF16), ((frames, voxels), BF16)],
        [pltpu.VMEM((cells * owned, LANES), F32)],
        name="prepare", inputs=3,
    )(movie, footprint, support_idx)
    resid, dense_in, proj_in = call(
        project_kernel,
        [((frames, voxels), BF16), ((3 * slots, voxels), BF16), ((slots, frames + LANES), F32)],
        [pltpu.VMEM((slots, support), jnp.int32), pltpu.VMEM((slots, support), F32), pltpu.VMEM((cells * slots, LANES), F32)],
        name="project", inputs=6,
    )(recv, movie_t, dense, trace_old, spatial, back_trace.reshape(1, frames))
    returned = exchange(proj_in, tiles)
    proj, energy, weight, base, impulse = call(
        own_kernel,
        [((owned, frames), F32), ((owned, LANES), F32), ((owned, LANES), F32), ((8, LANES), F32), ((frames, frames), F32)],
        name="own", smem=1, inputs=8,
    )(ar_coef, dense, resid, movie, spatial, footprint, send, pick_t)
    trace_new, send_new = call(
        trace_kernel,
        [((owned, frames), F32), ((slots, frames + LANES), F32)],
        name="trace", smem=1, inputs=10,
    )(ar_coef, returned, proj, energy, weight, base, impulse, trace_old, pick, pick_t)
    recv_new = exchange(send_new, tiles)
    total = jnp.sum(recv_new[:, frames:].reshape(tiles, CAP, LANES), axis=0)
    totals = [total] + [
        lax.ppermute(total, "region", [(i, (i + shift) % regions) for i in range(regions)])
        for shift in range(1, regions)
    ]
    rest = call(
        rest_kernel, [((frames, voxels), F32)], name="rest", inputs=5,
    )(recv_new, movie_t, dense, dense_in, trace_new)
    resid2, in_next, back = call(
        border_kernel,
        [((frames, voxels), BF16), ((slots, support), F32), ((2, LANES), F32)],
        [pltpu.VMEM((slots, voxels), F32), pltpu.VMEM((slots, support), jnp.int32), pltpu.VMEM((slots, support), F32)],
        name="border", inputs=4 + regions,
    )(recv, recv_new, *totals, spatial, rest)
    back_rows = exchange(in_next, tiles)
    footprint_new = call(
        footprint_kernel,
        [((owned, support), F32)],
        [pltpu.VMEM((owned, voxels), F32), pltpu.VMEM((owned, support), F32)],
        name="footprint", inputs=4,
    )(resid2, trace_new, footprint, support_idx)
    border_new = call(unpack_kernel, [((border, support), F32)], name="unpack", inputs=2)(place, back_rows)
    return (trace_new, footprint_new, border_new, back.reshape(frames))


def solution(mesh):
    row = P(("region", "tile"), None)
    flat = P(("region", "tile"))
    return jax.shard_map(
        body,
        mesh=mesh,
        in_specs=(row, row, row, row, P(), row, row, flat, row, flat, P()),
        out_specs=(row, row, row, P()),
        check_vma=False,
    )
```

```python
import jax
import jax.numpy as jnp
from jax import lax
from jax.experimental import pallas as pl
from jax.experimental.pallas import tpu as pltpu
from jax.sharding import PartitionSpec as P

CAP = 8
RIDGE = 1.0
LANES = 128
F32 = jnp.float32
BF16 = jnp.bfloat16
VMEM_BYTES = 40 << 20
CHUNK = 2048
TURN = 512
UNROLL = 64
PAD = 8


def nn(a, b):
    return lax.dot_general(a, b, (((1,), (0,)), ((), ())), preferred_element_type=F32)


def nt(a, b):
    return lax.dot_general(a, b, (((1,), (1,)), ((), ())), preferred_element_type=F32)


def split(x, terms):
    parts = []
    for _ in range(terms):
        part = x.astype(BF16)
        parts.append(part)
        x = x - part.astype(F32)
    return parts


def stack(table, terms=3):
    return jnp.concatenate([table] * terms, axis=1)


def select_rows(table, x, terms=3):
    return nn(stack(table, terms), jnp.concatenate(split(x, terms), axis=0))


def iota(shape, dim):
    return lax.broadcasted_iota(jnp.int32, shape, dim)


def to_column(row):
    n = row.shape[1]
    return jnp.sum(jnp.where(iota((n, n), 0) == iota((n, n), 1), row, jnp.zeros_like(row)), axis=1, keepdims=True)


def to_row(column):
    n = column.shape[0]
    return jnp.sum(jnp.where(iota((n, n), 0) == iota((n, n), 1), column, jnp.zeros_like(column)), axis=0, keepdims=True)


def shift_lanes(x, count):
    return jnp.where(iota(x.shape, len(x.shape) - 1) >= count, pltpu.roll(x, count, len(x.shape) - 1), 0.0)


def pieces(width):
    return [slice(start, start + CHUNK) for start in range(0, width, CHUNK)]


def fetch(source, target, sem):
    copy = pltpu.make_async_copy(source, target, sem)
    copy.start()
    return copy


def fetch_columns(*copies):
    return [
        [fetch(source.at[:, here], target.at[:, here], sems.at[k]) for source, target, sems in copies]
        for k, here in enumerate(pieces(copies[0][0].shape[1]))
    ]


def pack_kernel(tile_ref, bfp_hbm, bidx_hbm, bown_hbm, boff_hbm, old_hbm, send_ref, pick_ref, pick_t_ref, place_ref,
                bfp_ref, bidx_ref, bown_ref, boff_ref, old_ref, sems):
    copies = [
        fetch(source, target, sems.at[k])
        for k, (source, target) in enumerate(
            ((boff_hbm, boff_ref), (bown_hbm, bown_ref), (bfp_hbm, bfp_ref), (bidx_hbm, bidx_ref), (old_hbm, old_ref))
        )
    ]
    slots = send_ref.shape[0]
    tiles = slots // CAP
    border, support = bfp_ref.shape
    owned = old_ref.shape[0]
    copies[0].wait()
    copies[1].wait()
    target = boff_ref[...] + (tile_ref[0] + 1)
    target = jnp.where(target >= tiles, target - tiles, target)
    target_col = to_column(target)
    same = target_col == target
    before = iota((border, border), 0) < iota((border, border), 1)
    rank = jnp.sum(jnp.where(jnp.logical_and(same, before), 1, 0), axis=0, keepdims=True)
    slot = target * CAP + rank
    owner = bown_ref[...]
    place_t = iota((slots, border), 0) == slot
    place = iota((border, slots), 1) == to_column(slot)
    owner_col = jnp.sum(jnp.where(place_t, owner + 1, 0), axis=1, keepdims=True) - 1
    owner_row = jnp.sum(jnp.where(place, to_column(owner) + 1, 0), axis=0, keepdims=True) - 1
    pick = jnp.where(iota((slots, owned), 1) == owner_col, 1.0, 0.0).astype(BF16)
    pick_ref[...] = pick
    pick_t_ref[...] = jnp.where(iota((owned, slots), 0) == owner_row, 1.0, 0.0).astype(BF16)
    place_ref[...] = jnp.where(place, 1.0, 0.0).astype(BF16)
    place_t = jnp.where(place_t, 1.0, 0.0).astype(BF16)
    copies[2].wait()
    send_ref[:, :support] = select_rows(place_t, bfp_ref[...])
    copies[3].wait()
    send_ref[:, support:2 * support] = select_rows(place_t, bidx_ref[...].astype(F32), 2)
    copies[4].wait()
    send_ref[:, 2 * support:] = select_rows(pick, old_ref[...])


def scatter_rows(values_ref, index_ref, grid_ref, rows, stride, first=0):
    cells = grid_ref.shape[0] // stride
    support = values_ref.shape[1]
    hi_range = iota((cells, support), 0).astype(BF16)
    lo_range = iota((LANES, support), 0).astype(BF16)
    zero = jnp.zeros((cells, support), BF16)
    none = jnp.zeros((LANES, support), BF16)
    one = jnp.ones((LANES, support), BF16)

    def factors(row):
        index = index_ref[pl.ds(row, 1), :]
        value = values_ref[pl.ds(row, 1), :]
        high = jnp.broadcast_to((index >> 7).astype(F32), (cells, support)).astype(BF16)
        low = jnp.broadcast_to((index & 127).astype(F32), (LANES, support)).astype(BF16)
        coarse = value.astype(BF16).astype(F32)
        top = jnp.broadcast_to(coarse, (cells, support)).astype(BF16)
        rest = jnp.broadcast_to(value - coarse, (cells, support)).astype(BF16)
        hit = high == hi_range
        return jnp.where(hit, top, zero), jnp.where(hit, rest, zero), jnp.where(low == lo_range, one, none)

    for k in range(0, rows, 2):
        row = first + k
        top, rest, right = factors(row)
        top_next, rest_next, right_next = factors(row + 1)
        left = jnp.concatenate([
            jnp.concatenate([top, rest, zero, zero], axis=0),
            jnp.concatenate([zero, zero, top_next, rest_next], axis=0),
        ], axis=1)
        made = nt(left, jnp.concatenate([right, right_next], axis=1))
        grid_ref[pl.ds(k, cells, stride=stride), :] = made[:cells] + made[cells:2 * cells]
        grid_ref[pl.ds(k + 1, cells, stride=stride), :] = made[2 * cells:3 * cells] + made[3 * cells:]


def prepare_kernel(movie_hbm, fp_hbm, idx_hbm, dense_hbm, movie_t_hbm,
                   movie_ref, fp_ref, idx_ref, dense_ref, movie_t_ref, grid_ref, in_sems, movie_sems, dense_sems, out_sems):
    owned = fp_hbm.shape[0]
    voxels, frames = movie_hbm.shape
    groups = movie_sems.shape[0]
    rows = owned // groups
    width = voxels // groups
    stride = grid_ref.shape[0] // (voxels // LANES)
    loads = [fetch(fp_hbm, fp_ref, in_sems.at[0]), fetch(idx_hbm, idx_ref, in_sems.at[1])]
    for group in range(groups):
        fetch(movie_hbm.at[group * width:(group + 1) * width], movie_ref.at[group * width:(group + 1) * width], movie_sems.at[group])
    eye = jnp.where(iota((frames, frames), 0) == iota((frames, frames), 1), 1.0, 0.0).astype(BF16)
    for copy in loads:
        copy.wait()

    def parts(group):
        return pl.ds(pl.multiple_of(group * rows, rows), rows), pl.ds(pl.multiple_of(group * width, width), width)

    @pl.loop(0, groups)
    def _(group):
        mine, wide = parts(group)
        first = pl.multiple_of(group * rows, rows)
        scatter_rows(fp_ref, idx_ref, grid_ref, rows, stride, first)
        pltpu.make_async_copy(movie_hbm.at[wide], movie_ref.at[wide], movie_sems.at[group]).wait()
        for k in range(width // TURN):
            here = pl.ds(pl.multiple_of(group * width + k * TURN, TURN), TURN)
            movie_t_ref[:, here] = nt(eye, movie_ref[here, :]).astype(BF16)
        for cell in range(voxels // LANES):
            dense_ref[mine, cell * LANES:(cell + 1) * LANES] = grid_ref[cell * stride:cell * stride + rows, :].astype(BF16)
        fetch(dense_ref.at[mine], dense_hbm.at[mine], dense_sems.at[group])
        fetch(movie_t_ref.at[:, wide], movie_t_hbm.at[:, wide], out_sems.at[group])

    for group in range(groups):
        mine, wide = slice(group * rows, (group + 1) * rows), slice(group * width, (group + 1) * width)
        pltpu.make_async_copy(dense_ref.at[mine], dense_hbm.at[mine], dense_sems.at[group]).wait()
        pltpu.make_async_copy(movie_t_ref.at[:, wide], movie_t_hbm.at[:, wide], out_sems.at[group]).wait()


def transposed_parts(x):
    return jnp.concatenate([jnp.transpose(part.astype(F32)).astype(BF16) for part in split(x, 3)], axis=1)


def project_kernel(recv_ref, movie_t_hbm, dense_hbm, old_hbm, spatial_hbm, trace_hbm, resid_hbm, dense_in_hbm, proj_ref, weight_ref, base_ref,
                   movie_t_ref, dense_ref, old_ref, spatial_ref, trace_ref, resid_ref, values_ref, idx_ref,
                   grid_ref, in_sems, movie_sems, dense_sems, resid_sems, out_sem):
    slots = recv_ref.shape[0]
    owned = dense_hbm.shape[0]
    frames, voxels = movie_t_hbm.shape
    support = values_ref.shape[1]
    stride = slots + PAD
    first = [fetch(spatial_hbm, spatial_ref, in_sems.at[1]), fetch(old_hbm, old_ref, in_sems.at[0]), fetch(trace_hbm, trace_ref, in_sems.at[2])]
    loads = fetch_columns((dense_hbm, dense_ref.at[:owned], dense_sems), (movie_t_hbm, movie_t_ref, movie_sems))
    values_ref[...] = recv_ref[:, :support]
    idx_ref[...] = recv_ref[:, support:2 * support].astype(jnp.int32)
    scatter_rows(values_ref, idx_ref, grid_ref, slots, stride)
    for copy in first:
        copy.wait()
    both_t = jnp.concatenate([jnp.transpose(old_ref[...]).astype(BF16), transposed_parts(recv_ref[:, 2 * support:])], axis=1)
    back = to_column(trace_ref[...])
    seen_in = jnp.zeros((slots, LANES), F32)
    for cell in range(voxels // LANES):
        at = cell * LANES
        part = grid_ref[cell * stride:cell * stride + slots, :].astype(BF16)
        for copy in range(3):
            dense_ref[owned + copy * slots:owned + (copy + 1) * slots, at:at + LANES] = part
        seen_in += part.astype(F32) * spatial_ref[:, at:at + LANES]
    mine = dense_ref.at[owned:owned + slots]
    stores = [fetch(mine, dense_in_hbm, out_sem)]
    seen = jnp.zeros((frames, LANES), F32)
    weight = jnp.zeros((owned, LANES), F32)
    for k, here in enumerate(pieces(voxels)):
        for copy in loads[k]:
            copy.wait()
        recon = nn(both_t, dense_ref[:, here]) + back * spatial_ref[:, here]
        resid_ref[:, here] = (movie_t_ref[:, here].astype(F32) - recon).astype(BF16)
        for at in range(here.start, here.stop, LANES):
            profile = spatial_ref[:, at:at + LANES]
            seen += movie_t_ref[:, at:at + LANES].astype(F32) * profile
            weight += dense_ref[:owned, at:at + LANES].astype(F32) * profile
        stores.append(fetch(resid_ref.at[:, here], resid_hbm.at[:, here], resid_sems.at[k]))
    proj_ref[:, :frames] = nt(mine[...], resid_ref[...])
    proj_ref[:, frames:] = jnp.broadcast_to(jnp.sum(seen_in, axis=1, keepdims=True), (slots, LANES))
    weight_ref[...] = jnp.broadcast_to(jnp.sum(weight, axis=1, keepdims=True), (owned, LANES))
    seen = to_row(jnp.sum(seen, axis=1, keepdims=True))
    norm = jnp.sum(spatial_ref[...] * spatial_ref[...], axis=1, keepdims=True)
    row = iota((8, LANES), 0)
    base_ref[...] = jnp.where(row == 0, seen[:, :LANES], jnp.where(row == 1, seen[:, LANES:], jnp.where(row == 2, norm, 0.0)))
    for copy in stores:
        copy.wait()


def own_kernel(ar_ref, dense_hbm, resid_hbm, fp_hbm, old_hbm, send_ref, pick_t_ref, start_ref, scale_ref, impulse_ref,
               dense_ref, resid_ref, fp_ref, old_ref, in_sems):
    frames, voxels = resid_hbm.shape
    owned, support = fp_hbm.shape
    first = [fetch(fp_hbm, fp_ref, in_sems.at[0]), fetch(old_hbm, old_ref, in_sems.at[1])]
    dense_load = fetch(dense_hbm, dense_ref, in_sems.at[2])
    resid_load = fetch(resid_hbm, resid_ref, in_sems.at[3])
    near, far = ar_ref[0], ar_ref[1]
    response = jnp.where(iota((8, frames), 1) == 0, 1.0, 0.0)
    step = 1
    while step < frames:
        change = near * shift_lanes(response, step)
        if 2 * step < frames:
            change = change - far * shift_lanes(response, 2 * step)
        response = response + change
        near, far = near * near + 2.0 * far, -far * far
        step *= 2
    wide = jnp.broadcast_to(response[0:1], (frames, frames))
    wide = pltpu.roll(wide, 0, 1, stride=1, stride_axis=0)
    high, mid, low = split(jnp.where(iota((frames, frames), 1) >= iota((frames, frames), 0), wide, 0.0), 3)
    impulse_ref[...] = jnp.concatenate([high, mid, low, high, mid, high], axis=0)
    for copy in first:
        copy.wait()
    border_fp = send_ref[:, :support]
    square = jnp.broadcast_to(jnp.sum(border_fp * border_fp, axis=1, keepdims=True), (send_ref.shape[0], LANES))
    fp = fp_ref[...]
    share = 1.0 / (jnp.sum(fp * fp, axis=1, keepdims=True) + select_rows(pick_t_ref[...], square)[:, 0:1])
    scale_ref[...] = jnp.broadcast_to(share, (owned, LANES))
    dense_load.wait()
    resid_load.wait()
    start_ref[...] = old_ref[...] + nt(dense_ref[...], resid_ref[...]) * share


def trace_kernel(ar_ref, back_ref, start_ref, scale_ref, weight_ref, base_ref, impulse_ref, pick_ref, pick_t_ref, new_ref, send_ref):
    frames = start_ref.shape[1]
    returned = select_rows(pick_t_ref[...], back_ref[...])
    raw = start_ref[...] + returned[:, :frames] * scale_ref[:, 0:1]
    spikes = jnp.maximum(raw - ar_ref[0] * shift_lanes(raw, 1) - ar_ref[1] * shift_lanes(raw, 2), 0.0)
    high, mid, low = split(spikes, 3)
    new = nn(jnp.concatenate([high, high, high, mid, mid, low], axis=1), impulse_ref[...])
    new_ref[...] = new
    send_ref[:, :frames] = select_rows(pick_ref[...], new)
    used = weight_ref[:, 0:1] * new.astype(BF16).astype(F32) + returned[:, frames:frames + 1] * new
    used = jnp.sum(used, axis=0, keepdims=True)
    base = base_ref[...]
    row = iota((8, LANES), 0)
    base = base - jnp.where(row == 0, used[:, :LANES], jnp.where(row == 1, used[:, LANES:], 0.0))
    for tile in range(send_ref.shape[0] // CAP):
        send_ref[tile * CAP:(tile + 1) * CAP, frames:] = base


def rest_own_kernel(movie_t_hbm, dense_hbm, new_hbm, rest_hbm, movie_t_ref, dense_ref, new_ref, rest_ref, sem, movie_sems, dense_sems, out_sems):
    voxels = movie_t_hbm.shape[1]
    load = fetch(new_hbm, new_ref, sem)
    loads = fetch_columns((dense_hbm, dense_ref, dense_sems), (movie_t_hbm, movie_t_ref, movie_sems))
    load.wait()
    new_t = jnp.transpose(new_ref[...]).astype(BF16)
    stores = []
    for k, here in enumerate(pieces(voxels)):
        for copy in loads[k]:
            copy.wait()
        rest_ref[:, here] = movie_t_ref[:, here].astype(F32) - nn(new_t, dense_ref[:, here])
        stores.append(fetch(rest_ref.at[:, here], rest_hbm.at[:, here], out_sems.at[k]))
    for copy in stores:
        copy.wait()


def pick_support(grad_ref, idx_ref, out, rows):
    cells = grad_ref.shape[1] // LANES

    @pl.loop(0, rows // 64)
    def _(group):
        for k in range(8):
            here = pl.ds(pl.multiple_of(group * 64 + k * 8, 8), 8)
            index = idx_ref[here, :]
            high = index >> 7
            low = index & 127
            picked = jnp.zeros(index.shape, F32)
            for cell in range(cells):
                found = jnp.take_along_axis(grad_ref[here, cell * LANES:(cell + 1) * LANES], low, axis=1, mode="promise_in_bounds")
                picked = jnp.where(high == cell, found, picked)
            out(here, picked)


def rest_in_kernel(recv_ref, own_hbm, dense_in_hbm, rest_ref, own_ref, dense_in_ref, own_sems, *in_sems):
    slots = recv_ref.shape[0]
    frames, voxels = own_hbm.shape
    loads = fetch_columns(
        (own_hbm, own_ref, own_sems),
        *[(dense_in_hbm, dense_in_ref.at[copy * slots:(copy + 1) * slots], sems) for copy, sems in enumerate(in_sems)],
    )
    in_t = transposed_parts(recv_ref[:, :frames])
    for k, here in enumerate(pieces(voxels)):
        for copy in loads[k]:
            copy.wait()
        rest_ref[:, here] = own_ref[:, here] - nn(in_t, dense_in_ref[:, here])


def border_kernel(recv0_ref, recv_ref, *refs):
    *totals, spatial_hbm, rest_ref, resid_ref, next_ref, back_ref, spatial_ref, grad_ref, idx_ref, denom_ref, sem = refs
    frames, voxels = rest_ref.shape
    slots, support = next_ref.shape
    load = fetch(spatial_hbm, spatial_ref, sem)
    total = totals[0][...]
    for other in totals[1:]:
        total = total + other[...]
    back = total[0:2] / total[2:3, 0:1]
    back_ref[...] = back
    back = to_column(jnp.concatenate([back[0:1], back[1:2]], axis=1))
    new = recv_ref[:, :frames]
    idx_ref[...] = recv0_ref[:, support:2 * support].astype(jnp.int32)
    denom_ref[...] = jnp.broadcast_to(jnp.sum(new * new, axis=1, keepdims=True) + RIDGE, (slots, support))
    new_low = new.astype(BF16)
    load.wait()
    for here in pieces(voxels):
        resid = (rest_ref[:, here] - back * spatial_ref[:, here]).astype(BF16)
        resid_ref[:, here] = resid
        grad_ref[:, here] = nn(new_low, resid)

    def out(here, picked):
        next_ref[here, :] = jnp.maximum(recv0_ref[here, :support] + picked / denom_ref[here, :], 0.0)

    pick_support(grad_ref, idx_ref, out, slots)


def footprint_kernel(resid_ref, new_ref, fp_hbm, idx_hbm, out_ref, fp_ref, idx_ref, grad_ref, denom_ref, sems):
    frames, voxels = resid_ref.shape
    owned, support = fp_ref.shape
    first = [fetch(fp_hbm, fp_ref, sems.at[0]), fetch(idx_hbm, idx_ref, sems.at[1])]
    new = new_ref[...]
    new_low = new.astype(BF16)
    denom_ref[...] = jnp.broadcast_to(jnp.sum(new * new, axis=1, keepdims=True) + RIDGE, (owned, support))
    for here in pieces(voxels):
        grad_ref[:, here] = nn(new_low, resid_ref[:, here])
    for copy in first:
        copy.wait()

    def out(here, picked):
        out_ref[here, :] = jnp.maximum(fp_ref[here, :] + picked / denom_ref[here, :], 0.0)

    pick_support(grad_ref, idx_ref, out, owned)


def unpack_kernel(place_ref, rows_ref, out_ref):
    out_ref[...] = select_rows(place_ref[...], rows_ref[...])


def call(kernel, name, micros, ins, outs, scratch, *args):
    space = {"s": pltpu.SMEM, "v": pltpu.VMEM, "h": pltpu.HBM}
    shapes = [pltpu.HBM(shape, dtype) if where == "h" else jax.ShapeDtypeStruct(shape, dtype) for where, shape, dtype in outs]
    args = [pltpu.with_memory_space_constraint(arg, pltpu.HBM) if where == "h" else arg for where, arg in zip(ins, args)]
    places = [pl.BlockSpec(memory_space=space[where]) for where, _, _ in outs]
    many = len(outs) > 1
    return pl.pallas_call(
        kernel,
        out_shape=shapes if many else shapes[0],
        in_specs=[pl.BlockSpec(memory_space=space[where]) for where in ins],
        out_specs=places if many else places[0],
        scratch_shapes=list(scratch),
        cost_estimate=pl.CostEstimate(flops=0, bytes_accessed=int(micros * 3.5e6), transcendentals=0),
        compiler_params=pltpu.CompilerParams(vmem_limit_bytes=VMEM_BYTES),
        name=name,
    )(*args)


def exchange(rows, tiles):
    width = rows.shape[1]
    moved = lax.all_to_all(rows.reshape(tiles, CAP, width), "tile", split_axis=0, concat_axis=0, tiled=True)
    return moved.reshape(tiles * CAP, width)


def body(movie, footprint, support_idx, trace_old, ar_coef, border_fp, border_idx, border_owner, border_offset, back_spatial, back_trace):
    tiles = lax.axis_size("tile")
    regions = lax.axis_size("region")
    tile = lax.axis_index("tile").astype(jnp.int32).reshape(1)
    voxels, frames = movie.shape
    owned, support = footprint.shape
    border = border_fp.shape[0]
    slots = tiles * CAP
    cells = voxels // LANES
    spatial = back_spatial.reshape(1, voxels)
    V, dma, i32 = pltpu.VMEM, pltpu.SemaphoreType.DMA, jnp.int32
    n = voxels // CHUNK
    groups = owned // UNROLL
    wide = frames + LANES

    send, pick, pick_t, place = call(
        pack_kernel, "pack", 2, "shhhhh",
        [("v", (slots, 2 * support + frames), F32), ("v", (slots, owned), BF16), ("v", (owned, slots), BF16), ("v", (border, slots), BF16)],
        [V((border, support), F32), V((border, support), i32), V((1, border), i32), V((1, border), i32), V((owned, frames), F32), dma((5,))],
        tile, border_fp, border_idx, border_owner.reshape(1, border), border_offset.reshape(1, border), trace_old,
    )
    recv = exchange(send, tiles)
    dense, movie_t = call(
        prepare_kernel, "prepare", 7, "hhh",
        [("h", (owned, voxels), BF16), ("h", (frames, voxels), BF16)],
        [V((voxels, frames), BF16), V((owned, support), F32), V((owned, support), i32), V((owned, voxels), BF16), V((frames, voxels), BF16),
         V((cells * (UNROLL + PAD), LANES), F32), dma((2,)), dma((groups,)), dma((groups,)), dma((groups,))],
        movie, footprint, support_idx,
    )
    resid, dense_in, proj_in, weight, base = call(
        project_kernel, "project", 5, "vhhhhh",
        [("h", (frames, voxels), BF16), ("h", (slots, voxels), BF16), ("v", (slots, wide), F32), ("v", (owned, LANES), F32), ("v", (8, LANES), F32)],
        [V((frames, voxels), BF16), V((owned + 3 * slots, voxels), BF16), V((owned, frames), F32), V((1, voxels), F32), V((1, frames), F32),
         V((frames, voxels), BF16), V((slots, support), F32), V((slots, support), i32),
         V((cells * (slots + PAD), LANES), F32), dma((3,)), dma((n,)), dma((n,)), dma((n,)), dma],
        recv, movie_t, dense, trace_old, spatial, back_trace.reshape(1, frames),
    )
    returned = exchange(proj_in, tiles)
    start, scale, impulse = call(
        own_kernel, "own", 4, "shhhhvv",
        [("v", (owned, frames), F32), ("v", (owned, LANES), F32), ("v", (6 * frames, frames), BF16)],
        [V((owned, voxels), BF16), V((frames, voxels), BF16), V((owned, support), F32), V((owned, frames), F32), dma((4,))],
        ar_coef, dense, resid, footprint, trace_old, send, pick_t,
    )
    trace_new, send_new = call(
        trace_kernel, "trace", 2, "svvvvvvvv",
        [("v", (owned, frames), F32), ("v", (slots, wide), F32)], [],
        ar_coef, returned, start, scale, weight, base, impulse, pick, pick_t,
    )
    recv_new = exchange(send_new, tiles)
    rest_own = call(
        rest_own_kernel, "rest_own", 4, "hhh", [("h", (frames, voxels), F32)],
        [V((frames, voxels), BF16), V((owned, voxels), BF16), V((owned, frames), F32), V((frames, voxels), F32), dma, dma((n,)), dma((n,)), dma((n,))],
        movie_t, dense, trace_new,
    )
    recv_new, rest_own = lax.optimization_barrier((recv_new, rest_own))
    total = jnp.sum(recv_new[:, frames:].reshape(tiles, CAP, LANES), axis=0)
    totals = [total] + [
        lax.ppermute(total, "region", [(i, (i + shift) % regions) for i in range(regions)])
        for shift in range(1, regions)
    ]
    rest = call(
        rest_in_kernel, "rest_in", 4, "vhh", [("v", (frames, voxels), F32)],
        [V((frames, voxels), F32), V((3 * slots, voxels), BF16), dma((n,)), dma((n,)), dma((n,)), dma((n,))],
        recv_new, rest_own, dense_in,
    )
    resid2, in_next, back = call(
        border_kernel, "border", 3, "vv" + "v" * regions + "hv",
        [("v", (frames, voxels), BF16), ("v", (slots, support), F32), ("v", (2, LANES), F32)],
        [V((1, voxels), F32), V((slots, voxels), F32), V((slots, support), i32), V((slots, support), F32), dma],
        recv, recv_new, *totals, spatial, rest,
    )
    back_rows = exchange(in_next, tiles)
    footprint_new = call(
        footprint_kernel, "footprint", 4, "vvhh", [("v", (owned, support), F32)],
        [V((owned, support), F32), V((owned, support), i32), V((owned, voxels), F32), V((owned, support), F32), dma((2,))],
        resid2, trace_new, footprint, support_idx,
    )
    border_new = call(unpack_kernel, "unpack", 1, "vv", [("v", (border, support), F32)], [], place, back_rows)
    return (trace_new, footprint_new, border_new, back.reshape(frames))


def solution(mesh):
    row = P(("region", "tile"), None)
    flat = P(("region", "tile"))
    return jax.shard_map(
        body,
        mesh=mesh,
        in_specs=(row, row, row, row, P(), row, row, flat, row, flat, P()),
        out_specs=(row, row, row, P()),
        check_vma=False,
    )
```

```python
import jax
import jax.numpy as jnp
from jax import lax
from jax.experimental import pallas as pl
from jax.experimental.pallas import tpu as pltpu
from jax.sharding import PartitionSpec as P

CAP = 8
RIDGE = 1.0
LANES = 128
F32 = jnp.float32
BF16 = jnp.bfloat16
VMEM_BYTES = 40 << 20
CHUNK = 2048
TURN = 512
UNROLL = 128
PAD = 8


def nn(a, b):
    return lax.dot_general(a, b, (((1,), (0,)), ((), ())), preferred_element_type=F32)


def nt(a, b):
    return lax.dot_general(a, b, (((1,), (1,)), ((), ())), preferred_element_type=F32)


def split(x, terms):
    parts = []
    for _ in range(terms):
        part = x.astype(BF16)
        parts.append(part)
        x = x - part.astype(F32)
    return parts


def stack(table, terms=3):
    return jnp.concatenate([table] * terms, axis=1)


def select_rows(table, x, terms=3):
    return nn(stack(table, terms), jnp.concatenate(split(x, terms), axis=0))


def iota(shape, dim):
    return lax.broadcasted_iota(jnp.int32, shape, dim)


def to_column(row):
    n = row.shape[1]
    return jnp.sum(jnp.where(iota((n, n), 0) == iota((n, n), 1), row, jnp.zeros_like(row)), axis=1, keepdims=True)


def to_row(column):
    n = column.shape[0]
    return jnp.sum(jnp.where(iota((n, n), 0) == iota((n, n), 1), column, jnp.zeros_like(column)), axis=0, keepdims=True)


def shift_lanes(x, count):
    return jnp.where(iota(x.shape, len(x.shape) - 1) >= count, pltpu.roll(x, count, len(x.shape) - 1), 0.0)


def pieces(width):
    return [slice(start, start + CHUNK) for start in range(0, width, CHUNK)]


def fetch(source, target, sem):
    copy = pltpu.make_async_copy(source, target, sem)
    copy.start()
    return copy


def fetch_columns(*copies):
    return [
        [fetch(source.at[:, here], target.at[:, here], sems.at[k]) for source, target, sems in copies]
        for k, here in enumerate(pieces(copies[0][0].shape[1]))
    ]


def pack_kernel(tile_ref, bfp_hbm, bidx_hbm, bown_hbm, boff_hbm, old_hbm, fp_hbm, idx_hbm, send_ref, pick_ref, pick_t_ref, place_ref,
                fp_ref, idx_ref, bfp_ref, bidx_ref, bown_ref, boff_ref, old_ref, sems):
    copies = [
        fetch(source, target, sems.at[k])
        for k, (source, target) in enumerate(
            ((boff_hbm, boff_ref), (bown_hbm, bown_ref), (bfp_hbm, bfp_ref), (bidx_hbm, bidx_ref), (old_hbm, old_ref), (fp_hbm, fp_ref), (idx_hbm, idx_ref))
        )
    ]
    slots = send_ref.shape[0]
    tiles = slots // CAP
    border, support = bfp_ref.shape
    owned = old_ref.shape[0]
    copies[0].wait()
    copies[1].wait()
    target = boff_ref[...] + (tile_ref[0] + 1)
    target = jnp.where(target >= tiles, target - tiles, target)
    target_col = to_column(target)
    same = target_col == target
    before = iota((border, border), 0) < iota((border, border), 1)
    rank = jnp.sum(jnp.where(jnp.logical_and(same, before), 1, 0), axis=0, keepdims=True)
    slot = target * CAP + rank
    owner = bown_ref[...]
    place_t = iota((slots, border), 0) == slot
    place = iota((border, slots), 1) == to_column(slot)
    owner_col = jnp.sum(jnp.where(place_t, owner + 1, 0), axis=1, keepdims=True) - 1
    owner_row = jnp.sum(jnp.where(place, to_column(owner) + 1, 0), axis=0, keepdims=True) - 1
    pick = jnp.where(iota((slots, owned), 1) == owner_col, 1.0, 0.0).astype(BF16)
    pick_ref[...] = pick
    pick_t_ref[...] = jnp.where(iota((owned, slots), 0) == owner_row, 1.0, 0.0).astype(BF16)
    place_ref[...] = jnp.where(place, 1.0, 0.0).astype(BF16)
    place_t = jnp.where(place_t, 1.0, 0.0).astype(BF16)
    copies[2].wait()
    send_ref[:, :support] = select_rows(place_t, bfp_ref[...])
    copies[3].wait()
    send_ref[:, support:2 * support] = select_rows(place_t, bidx_ref[...].astype(F32), 2)
    copies[4].wait()
    send_ref[:, 2 * support:] = select_rows(pick, old_ref[...])
    copies[5].wait()
    copies[6].wait()


def scatter_rows(values_ref, index_ref, grid_ref, rows, stride, first=0):
    cells = grid_ref.shape[0] // stride
    support = values_ref.shape[1]
    hi_range = iota((cells, support), 0).astype(BF16)
    lo_range = iota((LANES, support), 0).astype(BF16)
    zero = jnp.zeros((cells, support), BF16)
    none = jnp.zeros((LANES, support), BF16)
    one = jnp.ones((LANES, support), BF16)

    def factors(row):
        index = index_ref[pl.ds(row, 1), :]
        value = values_ref[pl.ds(row, 1), :]
        high = jnp.broadcast_to((index >> 7).astype(F32), (cells, support)).astype(BF16)
        low = jnp.broadcast_to((index & 127).astype(F32), (LANES, support)).astype(BF16)
        coarse = value.astype(BF16).astype(F32)
        top = jnp.broadcast_to(coarse, (cells, support)).astype(BF16)
        rest = jnp.broadcast_to(value - coarse, (cells, support)).astype(BF16)
        hit = high == hi_range
        return jnp.where(hit, top, zero), jnp.where(hit, rest, zero), jnp.where(low == lo_range, one, none)

    for k in range(0, rows, 2):
        row = first + k
        top, rest, right = factors(row)
        top_next, rest_next, right_next = factors(row + 1)
        left = jnp.concatenate([
            jnp.concatenate([top, rest, zero, zero], axis=0),
            jnp.concatenate([zero, zero, top_next, rest_next], axis=0),
        ], axis=1)
        made = nt(left, jnp.concatenate([right, right_next], axis=1))
        grid_ref[pl.ds(k, cells, stride=stride), :] = made[:cells] + made[cells:2 * cells]
        grid_ref[pl.ds(k + 1, cells, stride=stride), :] = made[2 * cells:3 * cells] + made[3 * cells:]


def prepare_kernel(movie_hbm, fp_ref, idx_ref, spatial_hbm, dense_hbm, movie_t_hbm, seen_hbm,
                   movie_ref, dense_ref, movie_t_ref, grid_ref, spatial_ref, seen_ref, movie_sem, sems, dense_sems, out_sems):
    owned = fp_ref.shape[0]
    voxels, frames = movie_hbm.shape
    groups = dense_sems.shape[0]
    rows = owned // groups
    stride = grid_ref.shape[0] // (voxels // LANES)
    first = fetch(spatial_hbm, spatial_ref, sems.at[0])
    load = fetch(movie_hbm, movie_ref, movie_sem)
    eye = jnp.where(iota((frames, frames), 0) == iota((frames, frames), 1), 1.0, 0.0).astype(BF16)
    stores = []
    first.wait()
    for group in range(groups):
        mine = slice(group * rows, (group + 1) * rows)
        scatter_rows(fp_ref, idx_ref, grid_ref, rows, stride, group * rows)
        for start in range(mine.start, mine.stop, 8):
            seen_ref[start:start + 8, :] = pick_rows(spatial_ref, idx_ref[start:start + 8, :], slice(0, 1))
        for cell in range(voxels // LANES):
            dense_ref[mine, cell * LANES:(cell + 1) * LANES] = grid_ref[cell * stride:cell * stride + rows, :].astype(BF16)
        stores.append(fetch(dense_ref.at[mine], dense_hbm.at[mine], dense_sems.at[group]))
        if group == 0:
            load.wait()
            for k, here in enumerate(pieces(voxels)):
                movie_t_ref[:, here] = nt(eye, movie_ref[here, :]).astype(BF16)
                stores.append(fetch(movie_t_ref.at[:, here], movie_t_hbm.at[:, here], out_sems.at[k]))
    stores.append(fetch(seen_ref, seen_hbm, sems.at[1]))
    for copy in stores:
        copy.wait()


def transposed_parts(x):
    return jnp.concatenate([jnp.transpose(part.astype(F32)).astype(BF16) for part in split(x, 3)], axis=1)


def project_kernel(recv_ref, movie_t_hbm, dense_hbm, old_hbm, spatial_hbm, trace_hbm, resid_hbm, dense_in_hbm, proj_ref,
                   movie_t_ref, dense_ref, old_ref, spatial_ref, trace_ref, resid_ref, values_ref, idx_ref,
                   grid_ref, in_sems, movie_sems, dense_sems, resid_sems, out_sem):
    slots = recv_ref.shape[0]
    owned = dense_hbm.shape[0]
    frames, voxels = movie_t_hbm.shape
    support = values_ref.shape[1]
    stride = slots + PAD
    first = [fetch(spatial_hbm, spatial_ref, in_sems.at[1]), fetch(old_hbm, old_ref, in_sems.at[0]), fetch(trace_hbm, trace_ref, in_sems.at[2])]
    loads = fetch_columns((dense_hbm, dense_ref.at[:owned], dense_sems), (movie_t_hbm, movie_t_ref, movie_sems))
    values_ref[...] = recv_ref[:, :support]
    idx_ref[...] = recv_ref[:, support:2 * support].astype(jnp.int32)
    scatter_rows(values_ref, idx_ref, grid_ref, slots, stride)
    for copy in first:
        copy.wait()
    both_t = jnp.concatenate([jnp.transpose(old_ref[...]).astype(BF16), transposed_parts(recv_ref[:, 2 * support:])], axis=1)
    back = to_column(trace_ref[...])
    seen_in = jnp.zeros((slots, LANES), F32)
    for cell in range(voxels // LANES):
        at = cell * LANES
        part = grid_ref[cell * stride:cell * stride + slots, :].astype(BF16)
        for copy in range(3):
            dense_ref[owned + copy * slots:owned + (copy + 1) * slots, at:at + LANES] = part
        seen_in += part.astype(F32) * spatial_ref[:, at:at + LANES]
    mine = dense_ref.at[owned:owned + slots]
    stores = [fetch(mine, dense_in_hbm, out_sem)]
    for k, here in enumerate(pieces(voxels)):
        for copy in loads[k]:
            copy.wait()
        recon = nn(both_t, dense_ref[:, here]) + back * spatial_ref[:, here]
        resid_ref[:, here] = (movie_t_ref[:, here].astype(F32) - recon).astype(BF16)
        stores.append(fetch(resid_ref.at[:, here], resid_hbm.at[:, here], resid_sems.at[k]))
        part = nt(mine[:, here], resid_ref[:, here])
        total = part if k == 0 else total + part
    proj_ref[:, :frames] = total
    proj_ref[:, frames:] = jnp.broadcast_to(jnp.sum(seen_in, axis=1, keepdims=True), (slots, LANES))
    for copy in stores:
        copy.wait()


def own_kernel(ar_ref, dense_hbm, resid_hbm, movie_t_hbm, spatial_hbm, fp_hbm, old_hbm, send_ref, pick_t_ref, start_ref, scale_ref, weight_ref, base_ref, impulse_ref,
               dense_ref, resid_ref, movie_t_ref, spatial_ref, fp_ref, old_ref, in_sems):
    frames, voxels = resid_hbm.shape
    owned, support = fp_hbm.shape
    first = [fetch(fp_hbm, fp_ref, in_sems.at[0]), fetch(old_hbm, old_ref, in_sems.at[1]), fetch(spatial_hbm, spatial_ref, in_sems.at[4])]
    dense_load = fetch(dense_hbm, dense_ref, in_sems.at[2])
    movie_load = fetch(movie_t_hbm, movie_t_ref, in_sems.at[5])
    resid_load = fetch(resid_hbm, resid_ref, in_sems.at[3])
    near, far = ar_ref[0], ar_ref[1]
    response = jnp.where(iota((8, frames), 1) == 0, 1.0, 0.0)
    step = 1
    while step < frames:
        change = near * shift_lanes(response, step)
        if 2 * step < frames:
            change = change - far * shift_lanes(response, 2 * step)
        response = response + change
        near, far = near * near + 2.0 * far, -far * far
        step *= 2
    wide = jnp.broadcast_to(response[0:1], (frames, frames))
    wide = pltpu.roll(wide, 0, 1, stride=1, stride_axis=0)
    high, mid, low = split(jnp.where(iota((frames, frames), 1) >= iota((frames, frames), 0), wide, 0.0), 3)
    impulse_ref[...] = jnp.concatenate([high, mid, low, high, mid, high], axis=0)
    for copy in first:
        copy.wait()
    border_fp = send_ref[:, :support]
    square = jnp.broadcast_to(jnp.sum(border_fp * border_fp, axis=1, keepdims=True), (send_ref.shape[0], LANES))
    fp = fp_ref[...]
    share = 1.0 / (jnp.sum(fp * fp, axis=1, keepdims=True) + select_rows(pick_t_ref[...], square)[:, 0:1])
    scale_ref[...] = jnp.broadcast_to(share, (owned, LANES))
    dense_load.wait()
    weight = jnp.zeros((owned, LANES), F32)
    for at in range(0, voxels, LANES):
        weight += dense_ref[:, at:at + LANES].astype(F32) * spatial_ref[:, at:at + LANES]
    weight_ref[...] = jnp.broadcast_to(jnp.sum(weight, axis=1, keepdims=True), (owned, LANES))
    movie_load.wait()
    seen = jnp.zeros((frames, LANES), F32)
    for at in range(0, voxels, LANES):
        seen += movie_t_ref[:, at:at + LANES].astype(F32) * spatial_ref[:, at:at + LANES]
    seen = to_row(jnp.sum(seen, axis=1, keepdims=True))
    norm = jnp.sum(spatial_ref[...] * spatial_ref[...], axis=1, keepdims=True)
    row = iota((8, LANES), 0)
    base_ref[...] = jnp.where(row == 0, seen[:, :LANES], jnp.where(row == 1, seen[:, LANES:], jnp.where(row == 2, norm, 0.0)))
    resid_load.wait()
    start_ref[...] = old_ref[...] + nt(dense_ref[...], resid_ref[...]) * share


def trace_kernel(ar_ref, back_ref, start_ref, scale_ref, weight_ref, base_ref, impulse_ref, pick_ref, pick_t_ref, new_ref, send_ref, part_ref):
    frames = start_ref.shape[1]
    returned = select_rows(pick_t_ref[...], back_ref[...])
    raw = start_ref[...] + returned[:, :frames] * scale_ref[:, 0:1]
    spikes = jnp.maximum(raw - ar_ref[0] * shift_lanes(raw, 1) - ar_ref[1] * shift_lanes(raw, 2), 0.0)
    high, mid, low = split(spikes, 3)
    new = nn(jnp.concatenate([high, high, high, mid, mid, low], axis=1), impulse_ref[...])
    new_ref[...] = new
    send_ref[...] = select_rows(pick_ref[...], new)
    used = weight_ref[:, 0:1] * new.astype(BF16).astype(F32) + returned[:, frames:frames + 1] * new
    used = jnp.sum(used, axis=0, keepdims=True)
    base = base_ref[...]
    row = iota((8, LANES), 0)
    part_ref[...] = base - jnp.where(row == 0, used[:, :LANES], jnp.where(row == 1, used[:, LANES:], 0.0))


def pick_rows(grad_ref, index, rows):
    high = index >> 7
    low = index & 127
    picked = jnp.zeros(index.shape, F32)
    for cell in range(grad_ref.shape[1] // LANES):
        grad = jnp.broadcast_to(grad_ref[rows, cell * LANES:(cell + 1) * LANES], index.shape)
        found = jnp.take_along_axis(grad, low, axis=1, mode="promise_in_bounds")
        picked = jnp.where(high == cell, found, picked)
    return picked


def pick_support(grad_ref, idx_ref, out, rows):
    @pl.loop(0, rows // 64)
    def _(group):
        for k in range(8):
            here = pl.ds(pl.multiple_of(group * 64 + k * 8, 8), 8)
            out(here, pick_rows(grad_ref, idx_ref[here, :], slice(0, 1) if grad_ref.shape[0] == 1 else here))


def rest_own_kernel(movie_t_hbm, dense_hbm, new_hbm, spatial_hbm, trace_hbm, recv_ref, rest_hbm, seen_ref,
                    movie_t_ref, dense_ref, new_ref, spatial_ref, trace_ref, idx_ref, rest_ref, sems, movie_sems, dense_sems, out_sems):
    voxels = movie_t_hbm.shape[1]
    slots, support = idx_ref.shape
    first = [fetch(new_hbm, new_ref, sems.at[0]), fetch(spatial_hbm, spatial_ref, sems.at[1]), fetch(trace_hbm, trace_ref, sems.at[2])]
    loads = fetch_columns((dense_hbm, dense_ref, dense_sems), (movie_t_hbm, movie_t_ref, movie_sems))
    idx_ref[...] = recv_ref[:, support:2 * support].astype(jnp.int32)
    for copy in first:
        copy.wait()
    new_t = jnp.transpose(new_ref[...]).astype(BF16)
    back = to_column(trace_ref[...])
    stores = []
    for k, here in enumerate(pieces(voxels)):
        for copy in loads[k]:
            copy.wait()
        recon = nn(new_t, dense_ref[:, here]) + back * spatial_ref[:, here]
        rest_ref[:, here] = (movie_t_ref[:, here].astype(F32) - recon).astype(BF16)
        stores.append(fetch(rest_ref.at[:, here], rest_hbm.at[:, here], out_sems.at[k]))

    def out(here, picked):
        seen_ref[here, :] = picked

    pick_support(spatial_ref, idx_ref, out, slots)
    for copy in stores:
        copy.wait()


def against_rest(low, new):
    shared = nt(low, new.astype(BF16))
    for part in split(new, 3)[1:]:
        shared = shared + nt(low, part)
    return jnp.concatenate([low] + split(-shared, 2), axis=1)


def fetch_rest(rest_hbm, dense_in_hbm, both_ref, sems, in_sems):
    frames, slots = rest_hbm.shape[0], dense_in_hbm.shape[0]
    return fetch_columns(
        (rest_hbm, both_ref.at[:frames], sems),
        *[(dense_in_hbm, both_ref.at[frames + copy * slots:frames + (copy + 1) * slots], each) for copy, each in enumerate(in_sems)],
    )


def border_kernel(recv0_ref, recv_ref, seen_ref, *refs):
    *totals, rest_hbm, dense_in_hbm, send_ref, both_ref, grad_ref, idx_ref, sems, sems_near, sems_far = refs
    in_sems = (sems_near, sems_far)
    slots, support = seen_ref.shape
    loads = fetch_rest(rest_hbm, dense_in_hbm, both_ref, sems, in_sems)
    new = recv_ref[...]
    left = against_rest(new.astype(BF16), new)
    idx_ref[...] = recv0_ref[:, support:2 * support].astype(jnp.int32)
    send_ref[:, support:2 * support] = seen_ref[...]
    total = totals[0][...]
    for other in totals[1:]:
        total = total + other[...]
    for tile in range(slots // CAP):
        send_ref[tile * CAP:(tile + 1) * CAP, 2 * support:] = total
    for k, here in enumerate(pieces(both_ref.shape[1])):
        for copy in loads[k]:
            copy.wait()
        grad_ref[:, here] = nn(left, both_ref[:, here])

    def out(here, picked):
        send_ref[here, :support] = picked

    pick_support(grad_ref, idx_ref, out, slots)


def footprint_kernel(recv_ref, rest_hbm, dense_in_hbm, new_hbm, fp_hbm, idx_hbm, seen_hbm, send_hbm, send_new_hbm, trace_hbm,
                     base_ref, slope_ref, low_ref, border_ref, share_ref, sent_ref, old_ref,
                     both_ref, new_ref, fp_ref, idx_ref, seen_ref, send_ref, send_new_ref, grad_ref, part_ref, first_sems, sems, *in_sems):
    slots = recv_ref.shape[0]
    owned, support = fp_ref.shape
    first = [
        fetch(source, target, first_sems.at[k])
        for k, (source, target) in enumerate((
            (new_hbm, new_ref), (fp_hbm, fp_ref), (idx_hbm, idx_ref), (seen_hbm, seen_ref), (send_hbm, send_ref), (send_new_hbm, send_new_ref),
            (trace_hbm, old_ref),
        ))
    ]
    loads = fetch_rest(rest_hbm, dense_in_hbm, both_ref, sems, in_sems)
    for copy in first:
        copy.wait()
    new = new_ref[...]
    low = new.astype(BF16)
    low_ref[...] = low
    left = against_rest(low, recv_ref[...])
    part_ref[...] = jnp.broadcast_to(1.0 / (jnp.sum(new * new, axis=1, keepdims=True) + RIDGE), (owned, support))
    sent = send_new_ref[...]
    sent_ref[...] = sent.astype(BF16)
    share_ref[...] = jnp.broadcast_to(1.0 / (jnp.sum(sent * sent, axis=1, keepdims=True) + RIDGE), (slots, support))
    border_ref[...] = send_ref[:, :support]
    for k, here in enumerate(pieces(both_ref.shape[1])):
        for copy in loads[k]:
            copy.wait()
        grad_ref[:, here] = nn(left, both_ref[:, here])

    def out(here, picked):
        base_ref[here, :] = fp_ref[here, :] + picked * part_ref[here, :]
        slope_ref[here, :] = seen_ref[here, :] * part_ref[here, :]

    pick_support(grad_ref, idx_ref, out, owned)


def finish_kernel(rows_ref, base_ref, slope_ref, low_ref, border_ref, share_ref, sent_ref, old_ref, place_ref, out_ref, border_out_ref, back_ref):
    slots, support = border_ref.shape
    total = rows_ref[:CAP, 2 * support:]
    for tile in range(1, slots // CAP):
        total = total + rows_ref[tile * CAP:(tile + 1) * CAP, 2 * support:]
    back = total[0:2] / total[2:3, 0:1]
    back_ref[...] = back
    change = jnp.concatenate([back[0:1], back[1:2]], axis=1) - old_ref[...]
    along = jnp.sum(low_ref[...].astype(F32) * change, axis=1, keepdims=True)
    out_ref[...] = jnp.maximum(base_ref[...] - along * slope_ref[...], 0.0)
    along = jnp.sum(sent_ref[...].astype(F32) * change, axis=1, keepdims=True)
    grad = rows_ref[:, :support] - along * rows_ref[:, support:2 * support]
    border_out_ref[...] = select_rows(place_ref[...], jnp.maximum(border_ref[...] + grad * share_ref[...], 0.0))


def call(kernel, name, micros, ins, outs, scratch, *args):
    space = {"s": pltpu.SMEM, "v": pltpu.VMEM, "h": pltpu.HBM}
    shapes = [pltpu.HBM(shape, dtype) if where == "h" else jax.ShapeDtypeStruct(shape, dtype) for where, shape, dtype in outs]
    args = [pltpu.with_memory_space_constraint(arg, pltpu.HBM) if where == "h" else arg for where, arg in zip(ins, args)]
    places = [pl.BlockSpec(memory_space=space[where]) for where, _, _ in outs]
    many = len(outs) > 1
    return pl.pallas_call(
        kernel,
        out_shape=shapes if many else shapes[0],
        in_specs=[pl.BlockSpec(memory_space=space[where]) for where in ins],
        out_specs=places if many else places[0],
        scratch_shapes=list(scratch),
        cost_estimate=pl.CostEstimate(flops=0, bytes_accessed=int(micros * 3.5e6), transcendentals=0),
        compiler_params=pltpu.CompilerParams(vmem_limit_bytes=VMEM_BYTES),
        name=name,
    )(*args)


def exchange(rows, tiles):
    width = rows.shape[1]
    moved = lax.all_to_all(rows.reshape(tiles, CAP, width), "tile", split_axis=0, concat_axis=0, tiled=True)
    return moved.reshape(tiles * CAP, width)


def other_regions(total, regions):
    return [lax.ppermute(total, "region", [(i, (i + shift) % regions) for i in range(regions)]) for shift in range(1, regions)]


def body(movie, footprint, support_idx, trace_old, ar_coef, border_fp, border_idx, border_owner, border_offset, back_spatial, back_trace):
    tiles = lax.axis_size("tile")
    regions = lax.axis_size("region")
    tile = lax.axis_index("tile").astype(jnp.int32).reshape(1)
    voxels, frames = movie.shape
    owned, support = footprint.shape
    border = border_fp.shape[0]
    slots = tiles * CAP
    cells = voxels // LANES
    spatial = back_spatial.reshape(1, voxels)
    V, dma, i32 = pltpu.VMEM, pltpu.SemaphoreType.DMA, jnp.int32
    n = voxels // CHUNK
    groups = owned // UNROLL
    wide = frames + LANES

    send, pick, pick_t, place, footprint_near, support_near = call(
        pack_kernel, "pack", 2, "shhhhhhh",
        [("v", (slots, 2 * support + frames), F32), ("v", (slots, owned), BF16), ("v", (owned, slots), BF16), ("v", (border, slots), BF16),
         ("v", (owned, support), F32), ("v", (owned, support), i32)],
        [V((border, support), F32), V((border, support), i32), V((1, border), i32), V((1, border), i32), V((owned, frames), F32), dma((7,))],
        tile, border_fp, border_idx, border_owner.reshape(1, border), border_offset.reshape(1, border), trace_old, footprint, support_idx,
    )
    recv = exchange(send, tiles)
    dense, movie_t, seen_own = call(
        prepare_kernel, "prepare", 7, "hvvh",
        [("h", (owned, voxels), BF16), ("h", (frames, voxels), BF16), ("h", (owned, support), F32)],
        [V((voxels, frames), BF16), V((owned, voxels), BF16), V((frames, voxels), BF16),
         V((cells * (UNROLL + PAD), LANES), F32), V((1, voxels), F32), V((owned, support), F32), dma, dma((2,)), dma((groups,)), dma((n,))],
        movie, footprint_near, support_near, spatial,
    )
    resid, dense_in, proj_in = call(
        project_kernel, "project", 5, "vhhhhh",
        [("h", (frames, voxels), BF16), ("h", (slots, voxels), BF16), ("v", (slots, wide), F32)],
        [V((frames, voxels), BF16), V((owned + 3 * slots, voxels), BF16), V((owned, frames), F32), V((1, voxels), F32), V((1, frames), F32),
         V((frames, voxels), BF16), V((slots, support), F32), V((slots, support), i32),
         V((cells * (slots + PAD), LANES), F32), dma((3,)), dma((n,)), dma((n,)), dma((n,)), dma],
        recv, movie_t, dense, trace_old, spatial, back_trace.reshape(1, frames),
    )
    returned = exchange(proj_in, tiles)
    start, scale, weight, base, impulse = call(
        own_kernel, "own", 4, "shhhhhhvv",
        [("v", (owned, frames), F32), ("v", (owned, LANES), F32), ("v", (owned, LANES), F32), ("v", (CAP, LANES), F32), ("v", (6 * frames, frames), BF16)],
        [V((owned, voxels), BF16), V((frames, voxels), BF16), V((frames, voxels), BF16), V((1, voxels), F32), V((owned, support), F32),
         V((owned, frames), F32), dma((6,))],
        ar_coef, dense, resid, movie_t, spatial, footprint, trace_old, send, pick_t,
    )
    trace_new, send_new, part = call(
        trace_kernel, "trace", 2, "svvvvvvvv",
        [("v", (owned, frames), F32), ("v", (slots, frames), F32), ("v", (CAP, LANES), F32)], [],
        ar_coef, returned, start, scale, weight, base, impulse, pick, pick_t,
    )
    recv_new = exchange(send_new, tiles)
    totals = [part] + other_regions(part, regions)
    row_trace = back_trace.reshape(1, frames)
    rest, seen = call(
        rest_own_kernel, "rest_own", 4, "hhhhhv", [("h", (frames, voxels), BF16), ("v", (slots, support), F32)],
        [V((frames, voxels), BF16), V((owned, voxels), BF16), V((owned, frames), F32), V((1, voxels), F32), V((1, frames), F32), V((slots, support), i32),
         V((frames, voxels), BF16), dma((3,)), dma((n,)), dma((n,)), dma((n,))],
        movie_t, dense, trace_new, spatial, row_trace, recv,
    )
    recv_new, seen = lax.optimization_barrier((recv_new, seen))
    both = 2 * slots + frames
    send_back = call(
        border_kernel, "border", 4, "vvv" + "v" * regions + "hh", [("v", (slots, 2 * support + LANES), F32)],
        [V((both, voxels), BF16), V((slots, voxels), F32), V((slots, support), i32), dma((n,)), dma((n,)), dma((n,))],
        recv, recv_new, seen, *totals, rest, dense_in,
    )
    back_rows = exchange(send_back, tiles)
    parts = call(
        footprint_kernel, "footprint", 5, "vhhhhhhhhh",
        [("v", (owned, support), F32), ("v", (owned, support), F32), ("v", (owned, frames), BF16), ("v", (slots, support), F32), ("v", (slots, support), F32),
         ("v", (slots, frames), BF16), ("v", (1, frames), F32)],
        [V((both, voxels), BF16), V((owned, frames), F32), V((owned, support), F32), V((owned, support), i32), V((owned, support), F32),
         V((slots, 2 * support + frames), F32), V((slots, frames), F32), V((owned, voxels), F32), V((owned, support), F32),
         dma((7,)), dma((n,)), dma((n,)), dma((n,))],
        recv_new, rest, dense_in, trace_new, footprint, support_idx, seen_own, send, send_new, row_trace,
    )
    footprint_new, border_new, back = call(
        finish_kernel, "finish", 1, "vvvvvvvvv",
        [("v", (owned, support), F32), ("v", (border, support), F32), ("v", (2, LANES), F32)], [],
        back_rows, *parts, place,
    )
    return (trace_new, footprint_new, border_new, back.reshape(frames))


def solution(mesh):
    row = P(("region", "tile"), None)
    flat = P(("region", "tile"))
    return jax.shard_map(
        body,
        mesh=mesh,
        in_specs=(row, row, row, row, P(), row, row, flat, row, flat, P()),
        out_specs=(row, row, row, P()),
        check_vma=False,
    )
```

```python
import jax
import jax.numpy as jnp
from jax import lax
from jax.experimental import pallas as pl
from jax.experimental.pallas import tpu as pltpu
from jax.sharding import PartitionSpec as P

CAP = 8
RIDGE = 1.0
LANES = 128
F32 = jnp.float32
BF16 = jnp.bfloat16
VMEM_BYTES = 40 << 20
UNROLL = 128
PAD = 8


def nn(a, b):
    return lax.dot_general(a, b, (((1,), (0,)), ((), ())), preferred_element_type=F32)


def nt(a, b):
    return lax.dot_general(a, b, (((1,), (1,)), ((), ())), preferred_element_type=F32)


def split(x, terms):
    parts = []
    for _ in range(terms):
        part = x.astype(BF16)
        parts.append(part)
        x = x - part.astype(F32)
    return parts


def stack(table, terms=3):
    return jnp.concatenate([table] * terms, axis=1)


def select_rows(table, x, terms=3):
    return nn(stack(table, terms), jnp.concatenate(split(x, terms), axis=0))


def iota(shape, dim):
    return lax.broadcasted_iota(jnp.int32, shape, dim)


def to_column(row):
    n = row.shape[1]
    return jnp.sum(jnp.where(iota((n, n), 0) == iota((n, n), 1), row, jnp.zeros_like(row)), axis=1, keepdims=True)


def to_row(column):
    n = column.shape[0]
    return jnp.sum(jnp.where(iota((n, n), 0) == iota((n, n), 1), column, jnp.zeros_like(column)), axis=0, keepdims=True)


def shift_lanes(x, count):
    return jnp.where(iota(x.shape, len(x.shape) - 1) >= count, pltpu.roll(x, count, len(x.shape) - 1), 0.0)


def pieces(width, count):
    step = width // count
    return [slice(start, start + step) for start in range(0, width, step)]


def fetch(source, target, sem):
    copy = pltpu.make_async_copy(source, target, sem)
    copy.start()
    return copy


def fetch_columns(*copies):
    return [
        [fetch(source.at[:, here], target.at[:, here], sems.at[k]) for source, target, sems in copies]
        for k, here in enumerate(pieces(copies[0][0].shape[1], copies[0][2].shape[0]))
    ]


def pack_kernel(tile_ref, bfp_hbm, bidx_hbm, bown_hbm, boff_hbm, old_hbm, fp_hbm, idx_hbm, send_ref, pick_ref, pick_t_ref, place_ref,
                fp_ref, idx_ref, bfp_ref, bidx_ref, bown_ref, boff_ref, old_ref, sems):
    copies = [
        fetch(source, target, sems.at[k])
        for k, (source, target) in enumerate(
            ((boff_hbm, boff_ref), (bown_hbm, bown_ref), (bfp_hbm, bfp_ref), (bidx_hbm, bidx_ref), (old_hbm, old_ref), (fp_hbm, fp_ref), (idx_hbm, idx_ref))
        )
    ]
    slots = send_ref.shape[0]
    tiles = slots // CAP
    border, support = bfp_ref.shape
    owned = old_ref.shape[0]
    copies[0].wait()
    copies[1].wait()
    target = boff_ref[...] + (tile_ref[0] + 1)
    target = jnp.where(target >= tiles, target - tiles, target)
    target_col = to_column(target)
    same = target_col == target
    before = iota((border, border), 0) < iota((border, border), 1)
    rank = jnp.sum(jnp.where(jnp.logical_and(same, before), 1, 0), axis=0, keepdims=True)
    slot = target * CAP + rank
    owner = bown_ref[...]
    place_t = iota((slots, border), 0) == slot
    place = iota((border, slots), 1) == to_column(slot)
    owner_col = jnp.sum(jnp.where(place_t, owner + 1, 0), axis=1, keepdims=True) - 1
    owner_row = jnp.sum(jnp.where(place, to_column(owner) + 1, 0), axis=0, keepdims=True) - 1
    pick = jnp.where(iota((slots, owned), 1) == owner_col, 1.0, 0.0).astype(BF16)
    pick_ref[...] = pick
    pick_t_ref[...] = jnp.where(iota((owned, slots), 0) == owner_row, 1.0, 0.0).astype(BF16)
    place_ref[...] = jnp.where(place, 1.0, 0.0).astype(BF16)
    place_t = jnp.where(place_t, 1.0, 0.0).astype(BF16)
    copies[2].wait()
    send_ref[:, :support] = select_rows(place_t, bfp_ref[...])
    copies[3].wait()
    send_ref[:, support:2 * support] = select_rows(place_t, bidx_ref[...].astype(F32), 2)
    copies[4].wait()
    send_ref[:, 2 * support:] = select_rows(pick, old_ref[...])
    copies[5].wait()
    copies[6].wait()


def scatter_rows(values_ref, index_ref, grid_ref, cells, rows, stride, first=0):
    support = values_ref.shape[1]
    hi_range = iota((cells, support), 0).astype(BF16)
    lo_range = iota((LANES, support), 0).astype(BF16)
    zero = jnp.zeros((cells, support), BF16)
    none = jnp.zeros((LANES, support), BF16)
    one = jnp.ones((LANES, support), BF16)

    def factors(row):
        index = index_ref[pl.ds(row, 1), :]
        value = values_ref[pl.ds(row, 1), :]
        high = jnp.broadcast_to((index >> 7).astype(F32), (cells, support)).astype(BF16)
        low = jnp.broadcast_to((index & 127).astype(F32), (LANES, support)).astype(BF16)
        coarse = value.astype(BF16).astype(F32)
        top = jnp.broadcast_to(coarse, (cells, support)).astype(BF16)
        rest = jnp.broadcast_to(value - coarse, (cells, support)).astype(BF16)
        hit = high == hi_range
        return jnp.where(hit, top, zero), jnp.where(hit, rest, zero), jnp.where(low == lo_range, one, none)

    for k in range(0, rows, 2):
        row = first + k
        top, rest, right = factors(row)
        top_next, rest_next, right_next = factors(row + 1)
        left = jnp.concatenate([
            jnp.concatenate([top, rest, zero, zero], axis=0),
            jnp.concatenate([zero, zero, top_next, rest_next], axis=0),
        ], axis=1)
        made = nt(left, jnp.concatenate([right, right_next], axis=1))
        grid_ref[pl.ds(k, cells, stride=stride), :] = made[:cells] + made[cells:2 * cells]
        grid_ref[pl.ds(k + 1, cells, stride=stride), :] = made[2 * cells:3 * cells] + made[3 * cells:]


def prepare_kernel(movie_hbm, fp_ref, idx_ref, spatial_hbm, dense_hbm, movie_t_hbm, seen_hbm, movie_t_ref,
                   movie_ref, dense_ref, grid_ref, spatial_ref, seen_ref, movie_sem, sems, dense_sems, out_sems):
    owned = fp_ref.shape[0]
    voxels, frames = movie_hbm.shape
    groups = dense_sems.shape[0]
    rows = owned // groups
    cells = voxels // LANES
    stride = rows + PAD
    first = fetch(spatial_hbm, spatial_ref, sems.at[0])
    load = fetch(movie_hbm, movie_ref, movie_sem)
    eye = jnp.where(iota((frames, frames), 0) == iota((frames, frames), 1), 1.0, 0.0).astype(BF16)
    stores = []
    first.wait()
    for group in range(groups):
        mine = slice(group * rows, (group + 1) * rows)
        scatter_rows(fp_ref, idx_ref, grid_ref, cells, rows, stride, group * rows)
        for start in range(mine.start, mine.stop, 8):
            seen_ref[start:start + 8, :] = pick_rows(spatial_ref, idx_ref[start:start + 8, :], slice(0, 1))
        for cell in range(cells):
            dense_ref[mine, cell * LANES:(cell + 1) * LANES] = grid_ref[cell * stride:cell * stride + rows, :].astype(BF16)
        stores.append(fetch(dense_ref.at[mine], dense_hbm.at[mine], dense_sems.at[group]))
        if group == 0:
            load.wait()
            for k, here in enumerate(pieces(voxels, out_sems.shape[0])):
                movie_t_ref[:, here] = nt(eye, movie_ref[here, :]).astype(BF16)
                stores.append(fetch(movie_t_ref.at[:, here], movie_t_hbm.at[:, here], out_sems.at[k]))
    stores.append(fetch(seen_ref, seen_hbm, sems.at[1]))
    for copy in stores:
        copy.wait()


def transposed_parts(x):
    return jnp.concatenate([jnp.transpose(part.astype(F32)).astype(BF16) for part in split(x, 3)], axis=1)


def project_kernel(recv_ref, movie_t_ref, dense_hbm, old_hbm, spatial_hbm, trace_hbm, resid_hbm, dense_in_hbm, proj_ref,
                   dense_ref, old_ref, spatial_ref, trace_ref, resid_ref, values_ref, idx_ref,
                   grid_ref, in_sems, dense_sems, resid_sems, out_sem):
    slots = recv_ref.shape[0]
    owned = dense_hbm.shape[0]
    frames, voxels = movie_t_ref.shape
    support = values_ref.shape[1]
    stride = slots + PAD
    first = [fetch(spatial_hbm, spatial_ref, in_sems.at[1]), fetch(old_hbm, old_ref, in_sems.at[0]), fetch(trace_hbm, trace_ref, in_sems.at[2])]
    loads = fetch_columns((dense_hbm, dense_ref.at[:owned], dense_sems))
    in_t = transposed_parts(recv_ref[:, 2 * support:])
    values_ref[...] = recv_ref[:, :support]
    idx_ref[...] = recv_ref[:, support:2 * support].astype(jnp.int32)
    scatter_rows(values_ref, idx_ref, grid_ref, voxels // LANES, slots, stride)
    for copy in first:
        copy.wait()
    both_t = jnp.concatenate([jnp.transpose(old_ref[...]).astype(BF16), in_t], axis=1)
    back = to_column(trace_ref[...])
    seen_in = jnp.zeros((slots, LANES), F32)
    for cell in range(voxels // LANES):
        at = cell * LANES
        part = grid_ref[cell * stride:cell * stride + slots, :].astype(BF16)
        for copy in range(3):
            dense_ref[owned + copy * slots:owned + (copy + 1) * slots, at:at + LANES] = part
        seen_in += part.astype(F32) * spatial_ref[:, at:at + LANES]
    mine = dense_ref.at[owned:owned + slots]
    stores = [fetch(mine, dense_in_hbm, out_sem)]
    for k, here in enumerate(pieces(voxels, len(loads))):
        for copy in loads[k]:
            copy.wait()
        recon = nn(both_t, dense_ref[:, here]) + back * spatial_ref[:, here]
        resid_ref[:, here] = (movie_t_ref[:, here].astype(F32) - recon).astype(BF16)
        stores.append(fetch(resid_ref.at[:, here], resid_hbm.at[:, here], resid_sems.at[k]))
        part = nt(mine[:, here], resid_ref[:, here])
        total = part if k == 0 else total + part
    proj_ref[:, :frames] = total
    proj_ref[:, frames:] = jnp.broadcast_to(jnp.sum(seen_in, axis=1, keepdims=True), (slots, LANES))
    for copy in stores:
        copy.wait()


def own_kernel(ar_ref, dense_hbm, resid_hbm, movie_t_hbm, spatial_hbm, fp_hbm, old_hbm, send_ref, pick_t_ref, start_ref, scale_ref, weight_ref, base_ref, impulse_ref,
               dense_ref, resid_ref, movie_t_ref, spatial_ref, fp_ref, old_ref, in_sems):
    frames, voxels = resid_hbm.shape
    owned, support = fp_hbm.shape
    first = [fetch(fp_hbm, fp_ref, in_sems.at[0]), fetch(old_hbm, old_ref, in_sems.at[1]), fetch(spatial_hbm, spatial_ref, in_sems.at[4])]
    dense_load = fetch(dense_hbm, dense_ref, in_sems.at[2])
    movie_load = fetch(movie_t_hbm, movie_t_ref, in_sems.at[5])
    resid_load = fetch(resid_hbm, resid_ref, in_sems.at[3])
    near, far = ar_ref[0], ar_ref[1]
    response = jnp.where(iota((8, frames), 1) == 0, 1.0, 0.0)
    step = 1
    while step < frames:
        change = near * shift_lanes(response, step)
        if 2 * step < frames:
            change = change - far * shift_lanes(response, 2 * step)
        response = response + change
        near, far = near * near + 2.0 * far, -far * far
        step *= 2
    wide = jnp.broadcast_to(response[0:1], (frames, frames))
    wide = pltpu.roll(wide, 0, 1, stride=1, stride_axis=0)
    high, mid, low = split(jnp.where(iota((frames, frames), 1) >= iota((frames, frames), 0), wide, 0.0), 3)
    impulse_ref[...] = jnp.concatenate([high, mid, low, high, mid, high], axis=0)
    for copy in first:
        copy.wait()
    border_fp = send_ref[:, :support]
    square = jnp.broadcast_to(jnp.sum(border_fp * border_fp, axis=1, keepdims=True), (send_ref.shape[0], LANES))
    fp = fp_ref[...]
    share = 1.0 / (jnp.sum(fp * fp, axis=1, keepdims=True) + select_rows(pick_t_ref[...], square)[:, 0:1])
    scale_ref[...] = jnp.broadcast_to(share, (owned, LANES))
    dense_load.wait()
    weight = jnp.zeros((owned, LANES), F32)
    for at in range(0, voxels, LANES):
        weight += dense_ref[:, at:at + LANES].astype(F32) * spatial_ref[:, at:at + LANES]
    weight_ref[...] = jnp.broadcast_to(jnp.sum(weight, axis=1, keepdims=True), (owned, LANES))
    movie_load.wait()
    seen = jnp.zeros((frames, LANES), F32)
    for at in range(0, voxels, LANES):
        seen += movie_t_ref[:, at:at + LANES].astype(F32) * spatial_ref[:, at:at + LANES]
    seen = to_row(jnp.sum(seen, axis=1, keepdims=True))
    norm = jnp.sum(spatial_ref[...] * spatial_ref[...], axis=1, keepdims=True)
    row = iota((8, LANES), 0)
    base_ref[...] = jnp.where(row == 0, seen[:, :LANES], jnp.where(row == 1, seen[:, LANES:], jnp.where(row == 2, norm, 0.0)))
    resid_load.wait()
    start_ref[...] = old_ref[...] + nt(dense_ref[...], resid_ref[...]) * share


def trace_kernel(ar_ref, back_ref, start_ref, scale_ref, weight_ref, base_ref, impulse_ref, pick_ref, pick_t_ref, new_ref, send_ref, part_ref):
    frames = start_ref.shape[1]
    returned = select_rows(pick_t_ref[...], back_ref[...])
    raw = start_ref[...] + returned[:, :frames] * scale_ref[:, 0:1]
    spikes = jnp.maximum(raw - ar_ref[0] * shift_lanes(raw, 1) - ar_ref[1] * shift_lanes(raw, 2), 0.0)
    high, mid, low = split(spikes, 3)
    new = nn(jnp.concatenate([high, high, high, mid, mid, low], axis=1), impulse_ref[...])
    new_ref[...] = new
    send_ref[...] = select_rows(pick_ref[...], new)
    used = weight_ref[:, 0:1] * new.astype(BF16).astype(F32) + returned[:, frames:frames + 1] * new
    used = jnp.sum(used, axis=0, keepdims=True)
    base = base_ref[...]
    row = iota((8, LANES), 0)
    part_ref[...] = base - jnp.where(row == 0, used[:, :LANES], jnp.where(row == 1, used[:, LANES:], 0.0))


def pick_rows(grad_ref, index, rows):
    high = index >> 7
    low = index & 127
    picked = jnp.zeros(index.shape, F32)
    for cell in range(grad_ref.shape[1] // LANES):
        grad = jnp.broadcast_to(grad_ref[rows, cell * LANES:(cell + 1) * LANES], index.shape)
        found = jnp.take_along_axis(grad, low, axis=1, mode="promise_in_bounds")
        picked = jnp.where(high == cell, found, picked)
    return picked


def pick_support(grad_ref, idx_ref, out, rows):
    @pl.loop(0, rows // 64)
    def _(group):
        for k in range(8):
            here = pl.ds(pl.multiple_of(group * 64 + k * 8, 8), 8)
            out(here, pick_rows(grad_ref, idx_ref[here, :], slice(0, 1) if grad_ref.shape[0] == 1 else here))


def rest_own_kernel(movie_t_hbm, dense_hbm, new_hbm, spatial_hbm, trace_hbm, recv_ref, rest_hbm, seen_ref, rest_ref,
                    movie_t_ref, dense_ref, new_ref, spatial_ref, trace_ref, idx_ref, sems, movie_sems, dense_sems, out_sems):
    voxels = movie_t_hbm.shape[1]
    slots, support = idx_ref.shape
    first = [fetch(new_hbm, new_ref, sems.at[0]), fetch(spatial_hbm, spatial_ref, sems.at[1]), fetch(trace_hbm, trace_ref, sems.at[2])]
    loads = fetch_columns((dense_hbm, dense_ref, dense_sems), (movie_t_hbm, movie_t_ref, movie_sems))
    idx_ref[...] = recv_ref[:, support:2 * support].astype(jnp.int32)
    for copy in first:
        copy.wait()
    new_t = jnp.transpose(new_ref[...]).astype(BF16)
    back = to_column(trace_ref[...])
    stores = []
    for k, here in enumerate(pieces(voxels, len(loads))):
        for copy in loads[k]:
            copy.wait()
        recon = nn(new_t, dense_ref[:, here]) + back * spatial_ref[:, here]
        rest_ref[:, here] = (movie_t_ref[:, here].astype(F32) - recon).astype(BF16)
        stores.append(fetch(rest_ref.at[:, here], rest_hbm.at[:, here], out_sems.at[k]))

    def out(here, picked):
        seen_ref[here, :] = picked

    pick_support(spatial_ref, idx_ref, out, slots)
    for copy in stores:
        copy.wait()


def against_rest(low, new):
    shared = nt(low, new.astype(BF16))
    for part in split(new, 3)[1:]:
        shared = shared + nt(low, part)
    return jnp.concatenate([low] + split(-shared, 2), axis=1)


def fetch_rest(rest_hbm, dense_in_hbm, both_ref, sems, in_sems):
    frames, slots = rest_hbm.shape[0], dense_in_hbm.shape[0]
    return fetch_columns(
        (rest_hbm, both_ref.at[:frames], sems),
        *[(dense_in_hbm, both_ref.at[frames + copy * slots:frames + (copy + 1) * slots], each) for copy, each in enumerate(in_sems)],
    )


def border_kernel(recv0_ref, recv_ref, seen_ref, *refs):
    *totals, rest_ref, dense_in_hbm, send_ref, both_ref, grad_ref, idx_ref, sems = refs
    frames = rest_ref.shape[0]
    slots, support = seen_ref.shape
    loads = [fetch(dense_in_hbm, both_ref.at[copy * slots:(copy + 1) * slots], sems.at[copy]) for copy in range(2)]
    new = recv_ref[...]
    left = against_rest(new.astype(BF16), new)
    idx_ref[...] = recv0_ref[:, support:2 * support].astype(jnp.int32)
    send_ref[:, support:2 * support] = seen_ref[...]
    terms = [ref[...] for ref in totals]
    while len(terms) > 1:
        terms = [a + b for a, b in zip(terms[::2], terms[1::2])] + terms[len(terms) // 2 * 2:]
    total = terms[0]
    for tile in range(slots // CAP):
        send_ref[tile * CAP:(tile + 1) * CAP, 2 * support:] = total
    grad_ref[...] = nn(left[:, :frames], rest_ref[...])
    for copy in loads:
        copy.wait()
    grad_ref[...] += nn(left[:, frames:], both_ref[...])

    def out(here, picked):
        send_ref[here, :support] = picked

    pick_support(grad_ref, idx_ref, out, slots)


def footprint_kernel(recv_ref, rest_hbm, dense_in_hbm, new_hbm, fp_hbm, idx_hbm, seen_hbm, send_hbm, send_new_hbm, trace_hbm,
                     base_ref, slope_ref, low_ref, border_ref, share_ref, sent_ref, old_ref,
                     both_ref, new_ref, fp_ref, idx_ref, seen_ref, send_ref, send_new_ref, grad_ref, part_ref, first_sems, sems, *in_sems):
    slots = recv_ref.shape[0]
    owned, support = fp_ref.shape
    first = [
        fetch(source, target, first_sems.at[k])
        for k, (source, target) in enumerate((
            (new_hbm, new_ref), (fp_hbm, fp_ref), (idx_hbm, idx_ref), (seen_hbm, seen_ref), (send_hbm, send_ref), (send_new_hbm, send_new_ref),
            (trace_hbm, old_ref),
        ))
    ]
    loads = fetch_rest(rest_hbm, dense_in_hbm, both_ref, sems, in_sems)
    for copy in first:
        copy.wait()
    new = new_ref[...]
    low = new.astype(BF16)
    low_ref[...] = low
    left = against_rest(low, recv_ref[...])
    part_ref[...] = jnp.broadcast_to(1.0 / (jnp.sum(new * new, axis=1, keepdims=True) + RIDGE), (owned, support))
    sent = send_new_ref[...]
    sent_ref[...] = sent.astype(BF16)
    share_ref[...] = jnp.broadcast_to(1.0 / (jnp.sum(sent * sent, axis=1, keepdims=True) + RIDGE), (slots, support))
    border_ref[...] = send_ref[:, :support]
    for k, here in enumerate(pieces(both_ref.shape[1], len(loads))):
        for copy in loads[k]:
            copy.wait()
        grad_ref[:, here] = nn(left, both_ref[:, here])

    def out(here, picked):
        base_ref[here, :] = fp_ref[here, :] + picked * part_ref[here, :]
        slope_ref[here, :] = seen_ref[here, :] * part_ref[here, :]

    pick_support(grad_ref, idx_ref, out, owned)


def finish_kernel(rows_ref, base_ref, slope_ref, low_ref, border_ref, share_ref, sent_ref, old_ref, place_ref, out_ref, border_out_ref, back_ref):
    slots, support = border_ref.shape
    total = rows_ref[:CAP, 2 * support:]
    for tile in range(1, slots // CAP):
        total = total + rows_ref[tile * CAP:(tile + 1) * CAP, 2 * support:]
    back = total[0:2] / total[2:3, 0:1]
    back_ref[...] = back
    change = jnp.concatenate([back[0:1], back[1:2]], axis=1) - old_ref[...]
    along = jnp.sum(low_ref[...].astype(F32) * change, axis=1, keepdims=True)
    out_ref[...] = jnp.maximum(base_ref[...] - along * slope_ref[...], 0.0)
    along = jnp.sum(sent_ref[...].astype(F32) * change, axis=1, keepdims=True)
    grad = rows_ref[:, :support] - along * rows_ref[:, support:2 * support]
    border_out_ref[...] = select_rows(place_ref[...], jnp.maximum(border_ref[...] + grad * share_ref[...], 0.0))


def call(kernel, name, micros, ins, outs, scratch, *args):
    space = {"s": pltpu.SMEM, "v": pltpu.VMEM, "h": pltpu.HBM}
    shapes = [pltpu.HBM(shape, dtype) if where == "h" else jax.ShapeDtypeStruct(shape, dtype) for where, shape, dtype in outs]
    args = [pltpu.with_memory_space_constraint(arg, pltpu.HBM) if where == "h" else arg for where, arg in zip(ins, args)]
    places = [pl.BlockSpec(memory_space=space[where]) for where, _, _ in outs]
    many = len(outs) > 1
    return pl.pallas_call(
        kernel,
        out_shape=shapes if many else shapes[0],
        in_specs=[pl.BlockSpec(memory_space=space[where]) for where in ins],
        out_specs=places if many else places[0],
        scratch_shapes=list(scratch),
        cost_estimate=pl.CostEstimate(flops=0, bytes_accessed=int(micros * 3.5e6), transcendentals=0),
        compiler_params=pltpu.CompilerParams(vmem_limit_bytes=VMEM_BYTES),
        name=name,
    )(*args)


def exchange(rows, tiles):
    width = rows.shape[1]
    moved = lax.all_to_all(rows.reshape(tiles, CAP, width), "tile", split_axis=0, concat_axis=0, tiled=True)
    return moved.reshape(tiles * CAP, width)


def other_regions(total, regions):
    if regions & (regions - 1):
        return [lax.ppermute(total, "region", [(i, (i + shift) % regions) for i in range(regions)]) for shift in range(1, regions)]
    return [lax.ppermute(total, "region", [(i, i ^ mask) for i in range(regions)]) for mask in range(1, regions)]


def body(movie, footprint, support_idx, trace_old, ar_coef, border_fp, border_idx, border_owner, border_offset, back_spatial, back_trace):
    tiles = lax.axis_size("tile")
    regions = lax.axis_size("region")
    tile = lax.axis_index("tile").astype(jnp.int32).reshape(1)
    voxels, frames = movie.shape
    owned, support = footprint.shape
    border = border_fp.shape[0]
    slots = tiles * CAP
    cells = voxels // LANES
    spatial = back_spatial.reshape(1, voxels)
    V, dma, i32 = pltpu.VMEM, pltpu.SemaphoreType.DMA, jnp.int32
    groups = owned // UNROLL
    wide = frames + LANES

    send, pick, pick_t, place, footprint_near, support_near = call(
        pack_kernel, "pack", 2, "shhhhhhh",
        [("v", (slots, 2 * support + frames), F32), ("v", (slots, owned), BF16), ("v", (owned, slots), BF16), ("v", (border, slots), BF16),
         ("v", (owned, support), F32), ("v", (owned, support), i32)],
        [V((border, support), F32), V((border, support), i32), V((1, border), i32), V((1, border), i32), V((owned, frames), F32), dma((7,))],
        tile, border_fp, border_idx, border_owner.reshape(1, border), border_offset.reshape(1, border), trace_old, footprint, support_idx,
    )
    recv = exchange(send, tiles)
    dense, movie_t, seen_own, movie_near = call(
        prepare_kernel, "prepare", 7, "hvvh",
        [("h", (owned, voxels), BF16), ("h", (frames, voxels), BF16), ("h", (owned, support), F32), ("v", (frames, voxels), BF16)],
        [V((voxels, frames), BF16), V((owned, voxels), BF16),
         V(((cells + 1) * (UNROLL + PAD), LANES), F32), V((1, voxels), F32), V((owned, support), F32), dma, dma((2,)), dma((groups,)), dma((2,))],
        movie, footprint_near, support_near, spatial,
    )
    resid, dense_in, proj_in = call(
        project_kernel, "project", 5, "vvhhhh",
        [("h", (frames, voxels), BF16), ("h", (slots, voxels), BF16), ("v", (slots, wide), F32)],
        [V((owned + 3 * slots, voxels), BF16), V((owned, frames), F32), V((1, voxels), F32), V((1, frames), F32),
         V((frames, voxels), BF16), V((slots, support), F32), V((slots, support), i32),
         V(((cells + 1) * (slots + PAD), LANES), F32), dma((3,)), dma((2,)), dma((2,)), dma],
        recv, movie_near, dense, trace_old, spatial, back_trace.reshape(1, frames),
    )
    returned = exchange(proj_in, tiles)
    start, scale, weight, base, impulse = call(
        own_kernel, "own", 4, "shhhhhhvv",
        [("v", (owned, frames), F32), ("v", (owned, LANES), F32), ("v", (owned, LANES), F32), ("v", (CAP, LANES), F32), ("v", (6 * frames, frames), BF16)],
        [V((owned, voxels), BF16), V((frames, voxels), BF16), V((frames, voxels), BF16), V((1, voxels), F32), V((owned, support), F32),
         V((owned, frames), F32), dma((6,))],
        ar_coef, dense, resid, movie_t, spatial, footprint, trace_old, send, pick_t,
    )
    trace_new, send_new, part = call(
        trace_kernel, "trace", 2, "svvvvvvvv",
        [("v", (owned, frames), F32), ("v", (slots, frames), F32), ("v", (CAP, LANES), F32)], [],
        ar_coef, returned, start, scale, weight, base, impulse, pick, pick_t,
    )
    recv_new = exchange(send_new, tiles)
    totals = ([part] + other_regions(part, regions))[::-1]
    row_trace = back_trace.reshape(1, frames)
    rest, seen, rest_near = call(
        rest_own_kernel, "rest_own", 4, "hhhhhv", [("h", (frames, voxels), BF16), ("v", (slots, support), F32), ("v", (frames, voxels), BF16)],
        [V((frames, voxels), BF16), V((owned, voxels), BF16), V((owned, frames), F32), V((1, voxels), F32), V((1, frames), F32), V((slots, support), i32),
         dma((3,)), dma((2,)), dma((2,)), dma((2,))],
        movie_t, dense, trace_new, spatial, row_trace, recv,
    )
    recv_new, seen = lax.optimization_barrier((recv_new, seen))
    both = 2 * slots + frames
    send_back = call(
        border_kernel, "border", 4, "vvv" + "v" * regions + "vh", [("v", (slots, 2 * support + LANES), F32)],
        [V((2 * slots, voxels), BF16), V((slots, voxels), F32), V((slots, support), i32), dma((2,))],
        recv, recv_new, seen, *totals, rest_near, dense_in,
    )
    back_rows = exchange(send_back, tiles)
    parts = call(
        footprint_kernel, "footprint", 5, "vhhhhhhhhh",
        [("v", (owned, support), F32), ("v", (owned, support), F32), ("v", (owned, frames), BF16), ("v", (slots, support), F32), ("v", (slots, support), F32),
         ("v", (slots, frames), BF16), ("v", (1, frames), F32)],
        [V((both, voxels), BF16), V((owned, frames), F32), V((owned, support), F32), V((owned, support), i32), V((owned, support), F32),
         V((slots, 2 * support + frames), F32), V((slots, frames), F32), V((owned, voxels), F32), V((owned, support), F32),
         dma((7,)), dma((1,)), dma((1,)), dma((1,))],
        recv_new, rest, dense_in, trace_new, footprint, support_idx, seen_own, send, send_new, row_trace,
    )
    footprint_new, border_new, back = call(
        finish_kernel, "finish", 1, "vvvvvvvvv",
        [("v", (owned, support), F32), ("v", (border, support), F32), ("v", (2, LANES), F32)], [],
        back_rows, *parts, place,
    )
    return (trace_new, footprint_new, border_new, back.reshape(frames))


def solution(mesh):
    row = P(("region", "tile"), None)
    flat = P(("region", "tile"))
    return jax.shard_map(
        body,
        mesh=mesh,
        in_specs=(row, row, row, row, P(), row, row, flat, row, flat, P()),
        out_specs=(row, row, row, P()),
        check_vma=False,
    )
```

```python
import jax
import jax.numpy as jnp
from jax import lax
from jax.experimental import pallas as pl
from jax.experimental.pallas import tpu as pltpu
from jax.sharding import PartitionSpec as P

CAP = 8
RIDGE = 1.0
LANES = 128
F32 = jnp.float32
BF16 = jnp.bfloat16
VMEM_BYTES = 40 << 20
UNROLL = 128
PAD = 8


def nn(a, b):
    return lax.dot_general(a, b, (((1,), (0,)), ((), ())), preferred_element_type=F32)


def nt(a, b):
    return lax.dot_general(a, b, (((1,), (1,)), ((), ())), preferred_element_type=F32)


def split(x, terms):
    parts = []
    for _ in range(terms):
        part = x.astype(BF16)
        parts.append(part)
        x = x - part.astype(F32)
    return parts


def stack(table, terms=3):
    return jnp.concatenate([table] * terms, axis=1)


def select_rows(table, x, terms=3):
    return nn(stack(table, terms), jnp.concatenate(split(x, terms), axis=0))


def iota(shape, dim):
    return lax.broadcasted_iota(jnp.int32, shape, dim)


def to_column(row):
    n = row.shape[1]
    return jnp.sum(jnp.where(iota((n, n), 0) == iota((n, n), 1), row, jnp.zeros_like(row)), axis=1, keepdims=True)


def to_row(column):
    n = column.shape[0]
    return jnp.sum(jnp.where(iota((n, n), 0) == iota((n, n), 1), column, jnp.zeros_like(column)), axis=0, keepdims=True)


def shift_lanes(x, count):
    return jnp.where(iota(x.shape, len(x.shape) - 1) >= count, pltpu.roll(x, count, len(x.shape) - 1), 0.0)


def pieces(width, count):
    step = width // count
    return [slice(start, start + step) for start in range(0, width, step)]


def fetch(source, target, sem):
    copy = pltpu.make_async_copy(source, target, sem)
    copy.start()
    return copy


def fetch_columns(*copies):
    return [
        [fetch(source.at[:, here], target.at[:, here], sems.at[k]) for source, target, sems in copies]
        for k, here in enumerate(pieces(copies[0][0].shape[1], copies[0][2].shape[0]))
    ]


def pack_kernel(tile_ref, bfp_hbm, bidx_hbm, bown_hbm, boff_hbm, old_hbm, fp_hbm, idx_hbm, send_ref, pick_ref, pick_t_ref, place_ref,
                fp_ref, idx_ref, bfp_ref, bidx_ref, bown_ref, boff_ref, old_ref, sems):
    copies = [
        fetch(source, target, sems.at[k])
        for k, (source, target) in enumerate(
            ((boff_hbm, boff_ref), (bown_hbm, bown_ref), (bfp_hbm, bfp_ref), (bidx_hbm, bidx_ref), (old_hbm, old_ref), (fp_hbm, fp_ref), (idx_hbm, idx_ref))
        )
    ]
    slots = send_ref.shape[0]
    tiles = slots // CAP
    border, support = bfp_ref.shape
    owned = old_ref.shape[0]
    copies[0].wait()
    copies[1].wait()
    target = boff_ref[...] + (tile_ref[0] + 1)
    target = jnp.where(target >= tiles, target - tiles, target)
    target_col = to_column(target)
    same = target_col == target
    before = iota((border, border), 0) < iota((border, border), 1)
    rank = jnp.sum(jnp.where(jnp.logical_and(same, before), 1, 0), axis=0, keepdims=True)
    slot = target * CAP + rank
    owner = bown_ref[...]
    place_t = iota((slots, border), 0) == slot
    place = iota((border, slots), 1) == to_column(slot)
    owner_col = jnp.sum(jnp.where(place_t, owner + 1, 0), axis=1, keepdims=True) - 1
    owner_row = jnp.sum(jnp.where(place, to_column(owner) + 1, 0), axis=0, keepdims=True) - 1
    pick = jnp.where(iota((slots, owned), 1) == owner_col, 1.0, 0.0).astype(BF16)
    pick_ref[...] = pick
    pick_t_ref[...] = jnp.where(iota((owned, slots), 0) == owner_row, 1.0, 0.0).astype(BF16)
    place_ref[...] = jnp.where(place, 1.0, 0.0).astype(BF16)
    place_t = jnp.where(place_t, 1.0, 0.0).astype(BF16)
    copies[2].wait()
    send_ref[:, :support] = select_rows(place_t, bfp_ref[...])
    copies[3].wait()
    send_ref[:, support:2 * support] = select_rows(place_t, bidx_ref[...].astype(F32), 2)
    copies[4].wait()
    send_ref[:, 2 * support:] = select_rows(pick, old_ref[...])
    copies[5].wait()
    copies[6].wait()


def scatter_rows(values_ref, index_ref, grid_ref, cells, rows, stride, first=0):
    support = values_ref.shape[1]
    hi_range = iota((cells, support), 0).astype(BF16)
    lo_range = iota((LANES, support), 0).astype(BF16)
    zero = jnp.zeros((cells, support), BF16)
    none = jnp.zeros((LANES, support), BF16)
    one = jnp.ones((LANES, support), BF16)

    def factors(row):
        index = index_ref[pl.ds(row, 1), :]
        value = values_ref[pl.ds(row, 1), :]
        high = jnp.broadcast_to((index >> 7).astype(F32), (cells, support)).astype(BF16)
        low = jnp.broadcast_to((index & 127).astype(F32), (LANES, support)).astype(BF16)
        coarse = value.astype(BF16).astype(F32)
        top = jnp.broadcast_to(coarse, (cells, support)).astype(BF16)
        rest = jnp.broadcast_to(value - coarse, (cells, support)).astype(BF16)
        hit = high == hi_range
        return jnp.where(hit, top, zero), jnp.where(hit, rest, zero), jnp.where(low == lo_range, one, none)

    for k in range(0, rows, 2):
        row = first + k
        top, rest, right = factors(row)
        top_next, rest_next, right_next = factors(row + 1)
        left = jnp.concatenate([
            jnp.concatenate([top, rest, zero, zero], axis=0),
            jnp.concatenate([zero, zero, top_next, rest_next], axis=0),
        ], axis=1)
        made = nt(left, jnp.concatenate([right, right_next], axis=1))
        grid_ref[pl.ds(k, cells, stride=stride), :] = made[:cells] + made[cells:2 * cells]
        grid_ref[pl.ds(k + 1, cells, stride=stride), :] = made[2 * cells:3 * cells] + made[3 * cells:]


def prepare_kernel(movie_hbm, fp_ref, idx_ref, spatial_hbm, old_hbm, trace_hbm, dense_hbm, movie_t_hbm, seen_hbm, movie_t_ref, old_t_ref, back_ref,
                   movie_ref, dense_ref, grid_ref, spatial_ref, seen_ref, old_ref, trace_ref, movie_sem, sems, dense_sems, out_sems):
    owned = fp_ref.shape[0]
    voxels, frames = movie_hbm.shape
    groups = dense_sems.shape[0]
    rows = owned // groups
    cells = voxels // LANES
    stride = rows + PAD
    first = fetch(spatial_hbm, spatial_ref, sems.at[0])
    load = fetch(movie_hbm, movie_ref, movie_sem)
    later = [fetch(old_hbm, old_ref, sems.at[2]), fetch(trace_hbm, trace_ref, sems.at[3])]
    eye = jnp.where(iota((frames, frames), 0) == iota((frames, frames), 1), 1.0, 0.0).astype(BF16)
    stores = []
    first.wait()
    for group in range(groups):
        mine = slice(group * rows, (group + 1) * rows)
        scatter_rows(fp_ref, idx_ref, grid_ref, cells, rows, stride, group * rows)
        for start in range(mine.start, mine.stop, 8):
            seen_ref[start:start + 8, :] = pick_rows(spatial_ref, idx_ref[start:start + 8, :], slice(0, 1))
        for cell in range(cells):
            dense_ref[mine, cell * LANES:(cell + 1) * LANES] = grid_ref[cell * stride:cell * stride + rows, :].astype(BF16)
        stores.append(fetch(dense_ref.at[mine], dense_hbm.at[mine], dense_sems.at[group]))
        if group == 0:
            load.wait()
            for copy in later:
                copy.wait()
            old_t_ref[...] = jnp.transpose(old_ref[...]).astype(BF16)
            back_ref[...] = jnp.broadcast_to(to_column(trace_ref[...]), back_ref.shape)
            for k, here in enumerate(pieces(voxels, out_sems.shape[0])):
                movie_t_ref[:, here] = nt(eye, movie_ref[here, :]).astype(BF16)
                stores.append(fetch(movie_t_ref.at[:, here], movie_t_hbm.at[:, here], out_sems.at[k]))
    stores.append(fetch(seen_ref, seen_hbm, sems.at[1]))
    for copy in stores:
        copy.wait()


def transposed_parts(x):
    return jnp.concatenate([jnp.transpose(part.astype(F32)).astype(BF16) for part in split(x, 3)], axis=1)


def project_kernel(recv_ref, movie_t_ref, dense_hbm, old_t_ref, spatial_hbm, back_ref, resid_hbm, dense_in_hbm, proj_ref,
                   dense_ref, spatial_ref, resid_ref, values_ref, idx_ref,
                   grid_ref, in_sems, dense_sems, resid_sems, out_sem):
    slots = recv_ref.shape[0]
    owned = dense_hbm.shape[0]
    frames, voxels = movie_t_ref.shape
    support = values_ref.shape[1]
    stride = slots + PAD
    first = [fetch(spatial_hbm, spatial_ref, in_sems.at[0])]
    loads = fetch_columns((dense_hbm, dense_ref.at[:owned], dense_sems))
    in_t = transposed_parts(recv_ref[:, 2 * support:])
    values_ref[...] = recv_ref[:, :support]
    idx_ref[...] = recv_ref[:, support:2 * support].astype(jnp.int32)
    scatter_rows(values_ref, idx_ref, grid_ref, voxels // LANES, slots, stride)
    for copy in first:
        copy.wait()
    both_t = jnp.concatenate([old_t_ref[...], in_t], axis=1)
    back = back_ref[:, 0:1]
    seen_in = jnp.zeros((slots, LANES), F32)
    for cell in range(voxels // LANES):
        at = cell * LANES
        part = grid_ref[cell * stride:cell * stride + slots, :].astype(BF16)
        for copy in range(3):
            dense_ref[owned + copy * slots:owned + (copy + 1) * slots, at:at + LANES] = part
        seen_in += part.astype(F32) * spatial_ref[:, at:at + LANES]
    mine = dense_ref.at[owned:owned + slots]
    stores = [fetch(mine, dense_in_hbm, out_sem)]
    for k, here in enumerate(pieces(voxels, len(loads))):
        for copy in loads[k]:
            copy.wait()
        recon = nn(both_t, dense_ref[:, here]) + back * spatial_ref[:, here]
        resid_ref[:, here] = (movie_t_ref[:, here].astype(F32) - recon).astype(BF16)
        stores.append(fetch(resid_ref.at[:, here], resid_hbm.at[:, here], resid_sems.at[k]))
        part = nt(mine[:, here], resid_ref[:, here])
        total = part if k == 0 else total + part
    proj_ref[:, :frames] = total
    proj_ref[:, frames:] = jnp.broadcast_to(jnp.sum(seen_in, axis=1, keepdims=True), (slots, LANES))
    for copy in stores:
        copy.wait()


def own_kernel(ar_ref, dense_hbm, resid_hbm, movie_t_hbm, spatial_hbm, fp_hbm, old_hbm, send_ref, pick_t_ref, start_ref, scale_ref, weight_ref, base_ref, impulse_ref,
               dense_ref, resid_ref, movie_t_ref, spatial_ref, fp_ref, old_ref, in_sems):
    frames, voxels = resid_hbm.shape
    owned, support = fp_hbm.shape
    first = [fetch(fp_hbm, fp_ref, in_sems.at[0]), fetch(old_hbm, old_ref, in_sems.at[1]), fetch(spatial_hbm, spatial_ref, in_sems.at[4])]
    dense_load = fetch(dense_hbm, dense_ref, in_sems.at[2])
    movie_load = fetch(movie_t_hbm, movie_t_ref, in_sems.at[5])
    resid_load = fetch(resid_hbm, resid_ref, in_sems.at[3])
    near, far = ar_ref[0], ar_ref[1]
    response = jnp.where(iota((8, frames), 1) == 0, 1.0, 0.0)
    step = 1
    while step < frames:
        change = near * shift_lanes(response, step)
        if 2 * step < frames:
            change = change - far * shift_lanes(response, 2 * step)
        response = response + change
        near, far = near * near + 2.0 * far, -far * far
        step *= 2
    wide = jnp.broadcast_to(response[0:1], (frames, frames))
    wide = pltpu.roll(wide, 0, 1, stride=1, stride_axis=0)
    high, mid, low = split(jnp.where(iota((frames, frames), 1) >= iota((frames, frames), 0), wide, 0.0), 3)
    impulse_ref[...] = jnp.concatenate([high, mid, low, high, mid, high], axis=0)
    for copy in first:
        copy.wait()
    border_fp = send_ref[:, :support]
    square = jnp.broadcast_to(jnp.sum(border_fp * border_fp, axis=1, keepdims=True), (send_ref.shape[0], LANES))
    fp = fp_ref[...]
    share = 1.0 / (jnp.sum(fp * fp, axis=1, keepdims=True) + select_rows(pick_t_ref[...], square)[:, 0:1])
    scale_ref[...] = jnp.broadcast_to(share, (owned, LANES))
    dense_load.wait()
    weight = jnp.zeros((owned, LANES), F32)
    for at in range(0, voxels, LANES):
        weight += dense_ref[:, at:at + LANES].astype(F32) * spatial_ref[:, at:at + LANES]
    weight_ref[...] = jnp.broadcast_to(jnp.sum(weight, axis=1, keepdims=True), (owned, LANES))
    movie_load.wait()
    seen = jnp.zeros((frames, LANES), F32)
    for at in range(0, voxels, LANES):
        seen += movie_t_ref[:, at:at + LANES].astype(F32) * spatial_ref[:, at:at + LANES]
    seen = to_row(jnp.sum(seen, axis=1, keepdims=True))
    norm = jnp.sum(spatial_ref[...] * spatial_ref[...], axis=1, keepdims=True)
    row = iota((8, LANES), 0)
    base_ref[...] = jnp.where(row == 0, seen[:, :LANES], jnp.where(row == 1, seen[:, LANES:], jnp.where(row == 2, norm, 0.0)))
    resid_load.wait()
    start_ref[...] = old_ref[...] + nt(dense_ref[...], resid_ref[...]) * share


def trace_kernel(ar_ref, back_ref, start_ref, scale_ref, weight_ref, base_ref, impulse_ref, pick_ref, pick_t_ref, new_ref, send_ref, part_ref):
    frames = start_ref.shape[1]
    returned = select_rows(pick_t_ref[...], back_ref[...])
    raw = start_ref[...] + returned[:, :frames] * scale_ref[:, 0:1]
    spikes = jnp.maximum(raw - ar_ref[0] * shift_lanes(raw, 1) - ar_ref[1] * shift_lanes(raw, 2), 0.0)
    high, mid, low = split(spikes, 3)
    new = nn(jnp.concatenate([high, high, high, mid, mid, low], axis=1), impulse_ref[...])
    new_ref[...] = new
    send_ref[...] = select_rows(pick_ref[...], new)
    used = weight_ref[:, 0:1] * new.astype(BF16).astype(F32) + returned[:, frames:frames + 1] * new
    used = jnp.sum(used, axis=0, keepdims=True)
    base = base_ref[...]
    row = iota((8, LANES), 0)
    part_ref[...] = base - jnp.where(row == 0, used[:, :LANES], jnp.where(row == 1, used[:, LANES:], 0.0))


def pick_rows(grad_ref, index, rows):
    high = index >> 7
    low = index & 127
    picked = jnp.zeros(index.shape, F32)
    for cell in range(grad_ref.shape[1] // LANES):
        grad = jnp.broadcast_to(grad_ref[rows, cell * LANES:(cell + 1) * LANES], index.shape)
        found = jnp.take_along_axis(grad, low, axis=1, mode="promise_in_bounds")
        picked = jnp.where(high == cell, found, picked)
    return picked


def pick_support(grad_ref, idx_ref, out, rows):
    @pl.loop(0, rows // 64)
    def _(group):
        for k in range(8):
            here = pl.ds(pl.multiple_of(group * 64 + k * 8, 8), 8)
            out(here, pick_rows(grad_ref, idx_ref[here, :], slice(0, 1) if grad_ref.shape[0] == 1 else here))


def rest_own_kernel(movie_t_hbm, dense_hbm, new_hbm, spatial_hbm, trace_hbm, recv_ref, rest_hbm, seen_ref, rest_ref,
                    movie_t_ref, dense_ref, new_ref, spatial_ref, trace_ref, idx_ref, sems, movie_sems, dense_sems, out_sems):
    voxels = movie_t_hbm.shape[1]
    slots, support = idx_ref.shape
    first = [fetch(new_hbm, new_ref, sems.at[0]), fetch(spatial_hbm, spatial_ref, sems.at[1]), fetch(trace_hbm, trace_ref, sems.at[2])]
    loads = fetch_columns((dense_hbm, dense_ref, dense_sems), (movie_t_hbm, movie_t_ref, movie_sems))
    idx_ref[...] = recv_ref[:, support:2 * support].astype(jnp.int32)
    for copy in first:
        copy.wait()
    new_t = jnp.transpose(new_ref[...]).astype(BF16)
    back = to_column(trace_ref[...])
    stores = []
    for k, here in enumerate(pieces(voxels, len(loads))):
        for copy in loads[k]:
            copy.wait()
        recon = nn(new_t, dense_ref[:, here]) + back * spatial_ref[:, here]
        rest_ref[:, here] = (movie_t_ref[:, here].astype(F32) - recon).astype(BF16)
        stores.append(fetch(rest_ref.at[:, here], rest_hbm.at[:, here], out_sems.at[k]))

    def out(here, picked):
        seen_ref[here, :] = picked

    pick_support(spatial_ref, idx_ref, out, slots)
    for copy in stores:
        copy.wait()


def against_rest(low, new):
    shared = nt(low, new.astype(BF16))
    for part in split(new, 3)[1:]:
        shared = shared + nt(low, part)
    return jnp.concatenate([low] + split(-shared, 2), axis=1)


def fetch_rest(rest_hbm, dense_in_hbm, both_ref, sems, in_sems):
    frames, slots = rest_hbm.shape[0], dense_in_hbm.shape[0]
    return fetch_columns(
        (rest_hbm, both_ref.at[:frames], sems),
        *[(dense_in_hbm, both_ref.at[frames + copy * slots:frames + (copy + 1) * slots], each) for copy, each in enumerate(in_sems)],
    )


def border_kernel(recv0_ref, recv_ref, seen_ref, *refs):
    *totals, rest_ref, dense_in_hbm, send_ref, both_ref, grad_ref, idx_ref, sems = refs
    frames = rest_ref.shape[0]
    slots, support = seen_ref.shape
    loads = [fetch(dense_in_hbm, both_ref.at[copy * slots:(copy + 1) * slots], sems.at[copy]) for copy in range(2)]
    new = recv_ref[...]
    left = against_rest(new.astype(BF16), new)
    idx_ref[...] = recv0_ref[:, support:2 * support].astype(jnp.int32)
    send_ref[:, support:2 * support] = seen_ref[...]
    terms = [ref[...] for ref in totals]
    while len(terms) > 1:
        terms = [a + b for a, b in zip(terms[::2], terms[1::2])] + terms[len(terms) // 2 * 2:]
    total = terms[0]
    for tile in range(slots // CAP):
        send_ref[tile * CAP:(tile + 1) * CAP, 2 * support:] = total
    grad_ref[...] = nn(left[:, :frames], rest_ref[...])
    for copy in loads:
        copy.wait()
    grad_ref[...] += nn(left[:, frames:], both_ref[...])

    def out(here, picked):
        send_ref[here, :support] = picked

    pick_support(grad_ref, idx_ref, out, slots)


def footprint_kernel(recv_ref, rest_hbm, dense_in_hbm, new_hbm, fp_hbm, idx_hbm, seen_hbm, send_hbm, send_new_hbm, trace_hbm,
                     base_ref, slope_ref, low_ref, border_ref, share_ref, sent_ref, old_ref,
                     both_ref, new_ref, fp_ref, idx_ref, seen_ref, send_ref, send_new_ref, grad_ref, part_ref, first_sems, sems, *in_sems):
    slots = recv_ref.shape[0]
    owned, support = fp_ref.shape
    first = [
        fetch(source, target, first_sems.at[k])
        for k, (source, target) in enumerate((
            (new_hbm, new_ref), (fp_hbm, fp_ref), (idx_hbm, idx_ref), (seen_hbm, seen_ref), (send_hbm, send_ref), (send_new_hbm, send_new_ref),
            (trace_hbm, old_ref),
        ))
    ]
    loads = fetch_rest(rest_hbm, dense_in_hbm, both_ref, sems, in_sems)
    for copy in first:
        copy.wait()
    new = new_ref[...]
    low = new.astype(BF16)
    low_ref[...] = low
    left = against_rest(low, recv_ref[...])
    part_ref[...] = jnp.broadcast_to(1.0 / (jnp.sum(new * new, axis=1, keepdims=True) + RIDGE), (owned, support))
    sent = send_new_ref[...]
    sent_ref[...] = sent.astype(BF16)
    share_ref[...] = jnp.broadcast_to(1.0 / (jnp.sum(sent * sent, axis=1, keepdims=True) + RIDGE), (slots, support))
    border_ref[...] = send_ref[:, :support]
    for k, here in enumerate(pieces(both_ref.shape[1], len(loads))):
        for copy in loads[k]:
            copy.wait()
        grad_ref[:, here] = nn(left, both_ref[:, here])

    def out(here, picked):
        base_ref[here, :] = fp_ref[here, :] + picked * part_ref[here, :]
        slope_ref[here, :] = seen_ref[here, :] * part_ref[here, :]

    pick_support(grad_ref, idx_ref, out, owned)


def finish_kernel(rows_ref, base_ref, slope_ref, low_ref, border_ref, share_ref, sent_ref, old_ref, place_ref, out_ref, border_out_ref, back_ref):
    slots, support = border_ref.shape
    total = rows_ref[:CAP, 2 * support:]
    for tile in range(1, slots // CAP):
        total = total + rows_ref[tile * CAP:(tile + 1) * CAP, 2 * support:]
    back = total[0:2] / total[2:3, 0:1]
    back_ref[...] = back
    change = jnp.concatenate([back[0:1], back[1:2]], axis=1) - old_ref[...]
    along = jnp.sum(low_ref[...].astype(F32) * change, axis=1, keepdims=True)
    out_ref[...] = jnp.maximum(base_ref[...] - along * slope_ref[...], 0.0)
    along = jnp.sum(sent_ref[...].astype(F32) * change, axis=1, keepdims=True)
    grad = rows_ref[:, :support] - along * rows_ref[:, support:2 * support]
    border_out_ref[...] = select_rows(place_ref[...], jnp.maximum(border_ref[...] + grad * share_ref[...], 0.0))


def call(kernel, name, micros, ins, outs, scratch, *args):
    space = {"s": pltpu.SMEM, "v": pltpu.VMEM, "h": pltpu.HBM}
    shapes = [pltpu.HBM(shape, dtype) if where == "h" else jax.ShapeDtypeStruct(shape, dtype) for where, shape, dtype in outs]
    args = [pltpu.with_memory_space_constraint(arg, pltpu.HBM) if where == "h" else arg for where, arg in zip(ins, args)]
    places = [pl.BlockSpec(memory_space=space[where]) for where, _, _ in outs]
    many = len(outs) > 1
    return pl.pallas_call(
        kernel,
        out_shape=shapes if many else shapes[0],
        in_specs=[pl.BlockSpec(memory_space=space[where]) for where in ins],
        out_specs=places if many else places[0],
        scratch_shapes=list(scratch),
        cost_estimate=pl.CostEstimate(flops=0, bytes_accessed=int(micros * 3.5e6), transcendentals=0),
        compiler_params=pltpu.CompilerParams(vmem_limit_bytes=VMEM_BYTES),
        name=name,
    )(*args)


def exchange(rows, tiles):
    width = rows.shape[1]
    moved = lax.all_to_all(rows.reshape(tiles, CAP, width), "tile", split_axis=0, concat_axis=0, tiled=True)
    return moved.reshape(tiles * CAP, width)


def other_regions(total, regions):
    if regions & (regions - 1):
        return [lax.ppermute(total, "region", [(i, (i + shift) % regions) for i in range(regions)]) for shift in range(1, regions)]
    return [lax.ppermute(total, "region", [(i, i ^ mask) for i in range(regions)]) for mask in range(1, regions)]


def body(movie, footprint, support_idx, trace_old, ar_coef, border_fp, border_idx, border_owner, border_offset, back_spatial, back_trace):
    tiles = lax.axis_size("tile")
    regions = lax.axis_size("region")
    tile = lax.axis_index("tile").astype(jnp.int32).reshape(1)
    voxels, frames = movie.shape
    owned, support = footprint.shape
    border = border_fp.shape[0]
    slots = tiles * CAP
    cells = voxels // LANES
    spatial = back_spatial.reshape(1, voxels)
    V, dma, i32 = pltpu.VMEM, pltpu.SemaphoreType.DMA, jnp.int32
    groups = owned // UNROLL
    wide = frames + LANES

    send, pick, pick_t, place, footprint_near, support_near = call(
        pack_kernel, "pack", 2, "shhhhhhh",
        [("v", (slots, 2 * support + frames), F32), ("v", (slots, owned), BF16), ("v", (owned, slots), BF16), ("v", (border, slots), BF16),
         ("v", (owned, support), F32), ("v", (owned, support), i32)],
        [V((border, support), F32), V((border, support), i32), V((1, border), i32), V((1, border), i32), V((owned, frames), F32), dma((7,))],
        tile, border_fp, border_idx, border_owner.reshape(1, border), border_offset.reshape(1, border), trace_old, footprint, support_idx,
    )
    recv = exchange(send, tiles)
    dense, movie_t, seen_own, movie_near, old_t, back_column = call(
        prepare_kernel, "prepare", 7, "hvvhhh",
        [("h", (owned, voxels), BF16), ("h", (frames, voxels), BF16), ("h", (owned, support), F32), ("v", (frames, voxels), BF16),
         ("v", (frames, owned), BF16), ("v", (frames, LANES), F32)],
        [V((voxels, frames), BF16), V((owned, voxels), BF16),
         V(((cells + 1) * (UNROLL + PAD), LANES), F32), V((1, voxels), F32), V((owned, support), F32), V((owned, frames), F32), V((1, frames), F32), dma, dma((4,)), dma((groups,)), dma((2,))],
        movie, footprint_near, support_near, spatial, trace_old, back_trace.reshape(1, frames),
    )
    resid, dense_in, proj_in = call(
        project_kernel, "project", 5, "vvhvhv",
        [("h", (frames, voxels), BF16), ("h", (slots, voxels), BF16), ("v", (slots, wide), F32)],
        [V((owned + 3 * slots, voxels), BF16), V((1, voxels), F32),
         V((frames, voxels), BF16), V((slots, support), F32), V((slots, support), i32),
         V(((cells + 1) * (slots + PAD), LANES), F32), dma((1,)), dma((2,)), dma((2,)), dma],
        recv, movie_near, dense, old_t, spatial, back_column,
    )
    returned = exchange(proj_in, tiles)
    start, scale, weight, base, impulse = call(
        own_kernel, "own", 4, "shhhhhhvv",
        [("v", (owned, frames), F32), ("v", (owned, LANES), F32), ("v", (owned, LANES), F32), ("v", (CAP, LANES), F32), ("v", (6 * frames, frames), BF16)],
        [V((owned, voxels), BF16), V((frames, voxels), BF16), V((frames, voxels), BF16), V((1, voxels), F32), V((owned, support), F32),
         V((owned, frames), F32), dma((6,))],
        ar_coef, dense, resid, movie_t, spatial, footprint, trace_old, send, pick_t,
    )
    trace_new, send_new, part = call(
        trace_kernel, "trace", 2, "svvvvvvvv",
        [("v", (owned, frames), F32), ("v", (slots, frames), F32), ("v", (CAP, LANES), F32)], [],
        ar_coef, returned, start, scale, weight, base, impulse, pick, pick_t,
    )
    recv_new = exchange(send_new, tiles)
    totals = ([part] + other_regions(part, regions))[::-1]
    row_trace = back_trace.reshape(1, frames)
    rest, seen, rest_near = call(
        rest_own_kernel, "rest_own", 4, "hhhhhv", [("h", (frames, voxels), BF16), ("v", (slots, support), F32), ("v", (frames, voxels), BF16)],
        [V((frames, voxels), BF16), V((owned, voxels), BF16), V((owned, frames), F32), V((1, voxels), F32), V((1, frames), F32), V((slots, support), i32),
         dma((3,)), dma((2,)), dma((2,)), dma((2,))],
        movie_t, dense, trace_new, spatial, row_trace, recv,
    )
    recv_new, seen = lax.optimization_barrier((recv_new, seen))
    both = 2 * slots + frames
    send_back = call(
        border_kernel, "border", 4, "vvv" + "v" * regions + "vh", [("v", (slots, 2 * support + LANES), F32)],
        [V((2 * slots, voxels), BF16), V((slots, voxels), F32), V((slots, support), i32), dma((2,))],
        recv, recv_new, seen, *totals, rest_near, dense_in,
    )
    back_rows = exchange(send_back, tiles)
    parts = call(
        footprint_kernel, "footprint", 5, "vhhhhhhhhh",
        [("v", (owned, support), F32), ("v", (owned, support), F32), ("v", (owned, frames), BF16), ("v", (slots, support), F32), ("v", (slots, support), F32),
         ("v", (slots, frames), BF16), ("v", (1, frames), F32)],
        [V((both, voxels), BF16), V((owned, frames), F32), V((owned, support), F32), V((owned, support), i32), V((owned, support), F32),
         V((slots, 2 * support + frames), F32), V((slots, frames), F32), V((owned, voxels), F32), V((owned, support), F32),
         dma((7,)), dma((1,)), dma((1,)), dma((1,))],
        recv_new, rest, dense_in, trace_new, footprint, support_idx, seen_own, send, send_new, row_trace,
    )
    footprint_new, border_new, back = call(
        finish_kernel, "finish", 1, "vvvvvvvvv",
        [("v", (owned, support), F32), ("v", (border, support), F32), ("v", (2, LANES), F32)], [],
        back_rows, *parts, place,
    )
    return (trace_new, footprint_new, border_new, back.reshape(frames))


def solution(mesh):
    row = P(("region", "tile"), None)
    flat = P(("region", "tile"))
    return jax.shard_map(
        body,
        mesh=mesh,
        in_specs=(row, row, row, row, P(), row, row, flat, row, flat, P()),
        out_specs=(row, row, row, P()),
        check_vma=False,
    )
```
